32 devices in a mesh: grp: 2 (over x), ty: 16 (over z, y, core).
Axes of the slice: x: 2, y: 2, z: 4, core: 2. Of those that a mesh axis runs over, the one named last changes fastest.
Arguments:
- tile_object: float32 [4, 2, 4096, 768], P(None, None, ('grp', 'ty')), parts along dimension 2, may hold values from -6 to 6
- probe_wave: float32 [2, 128, 128], replicated, may hold values from -6 to 6
- propagator_phase: float32 [128, 128], replicated, may hold values from -3.140625 to 3.140625
- diffraction: float32 [128, 128, 128], P(('grp', 'ty')), parts along dimension 0, may hold values from 0 to 2
- positions: int32 [128, 2], P(('grp', 'ty')), parts along dimension 0, may hold values from 0 to 640, as said below
- counts: int32 [32], P(('grp', 'ty')), parts along dimension 0, may hold values from 0 to 4, as said below
Outputs:
- object_grad: float32 [4, 2, 4096, 768], P(None, None, ('grp', 'ty')), parts along dimension 2
The draws below stay inside these ranges and needn't reach their ends.
There are 2 independent parts, one for each index of `grp`. The reference program is written for one: setup_inputs(seed, part) draws one part's arguments, and reference() takes and returns one part's arrays. A program takes and returns all parts, laid end to end along the dimension named above; an argument that names none is the same for every part. Nothing has to cross between parts.
Inputs may be any that keep to these rules, and one draw needn't show every extreme that they name: `positions`: column 0 is a row offset under 128, column 1 a column offset of at most 640. For every device d, the counts of devices 0 to d sum to between 2 * (d + 1) and 2 * (d + 2), the upper bound reached at some device; all counts sum to 32.
All inputs are finite; a program needn't handle non-finite values.
Results may differ from the reference program's by a relative error of at most 0.0003.
Values sent between devices are 32-bit elements; how exact they have to be, the bound alone decides.
A program may use at most 64 MiB of HBM per device.

```python
import jax
import jax.numpy as jnp
from jax import lax

PS = 128
NS = 4
TR = 128
OW = 768
BATCH = 2
SLOTS = 4
TILES = 16
SLOTS_ALL = 64
OROWS = 2048


def draw_counts(key, part):
    surplus = jax.random.randint(jax.random.fold_in(key, 11), (TILES,), 0, BATCH + 1)
    marker = jax.random.randint(jax.random.fold_in(key, 12), (), 0, TILES - 2)
    indices = jnp.arange(TILES)
    surplus = jnp.where(indices == marker, BATCH, surplus)
    cleared = (indices == marker - 1) | (indices == marker + 1) | (indices == TILES - 1)
    surplus = jnp.where(cleared, 0, surplus)
    before = jnp.concatenate([jnp.zeros((1,), surplus.dtype), surplus[:-1]])
    return (BATCH + surplus - before).astype(jnp.int32)


def draw_positions(key, part):
    rows_drawn = jax.random.randint(jax.random.fold_in(key, 21), (SLOTS_ALL,), 0, TR)
    cols_drawn = jax.random.randint(jax.random.fold_in(key, 22), (SLOTS_ALL,), 0, OW - PS + 1)
    chosen = jax.random.randint(jax.random.fold_in(key, 23), (), 0, SLOTS_ALL)
    indices = jnp.arange(SLOTS_ALL)
    rows_drawn = jnp.where(indices == chosen, TR - 1, rows_drawn)
    cols_drawn = jnp.where(indices == chosen, OW - PS, cols_drawn)
    return jnp.stack([rows_drawn, cols_drawn], axis=1).astype(jnp.int32)


def block_scale(key, shape, shards, smallest, top_value):
    gain = 1.0
    for axis_at, blocks in shards:
        draws = jax.random.uniform(jax.random.fold_in(jax.random.fold_in(key, 6), axis_at), (blocks,), jnp.float32, smallest / len(shards), top_value / len(shards))
        gain = gain * jnp.repeat(jnp.exp(draws), shape[axis_at] // blocks).reshape((-1,) + (1,) * (len(shape) - 1 - axis_at))
    return gain


def scatter_about(rng, extent, scale, bound, shards=(), kind=jnp.bfloat16):
    entries = jax.random.normal(rng, extent, jnp.float32) * scale
    if len(shards) > 0:
        entries = block_scale(rng, extent, shards, -0.22, 0.18) * entries
    return jnp.clip(entries, min=-bound, max=bound).astype(kind)


def setup_inputs(seed: int = 0, part: int = 0) -> dict:
    streams_of = jax.random.split(jax.random.key(seed), 7)
    part_keys = jax.random.split(jax.random.fold_in(streams_of[6], part), 7)
    tile_object = scatter_about(part_keys[0], (NS, 2, OROWS, OW), 0.7, 6.0, ((2, 16),), jnp.float32)
    probe_wave = scatter_about(streams_of[1], (2, PS, PS), 0.7, 6.0, (), jnp.float32)
    propagator_phase = jnp.clip(jax.random.uniform(streams_of[2], (PS, PS), jnp.float32, -3.140625, 3.140625), -3.140625, 3.140625)
    diffraction = jnp.clip(2.0 * jax.random.uniform(part_keys[3], (SLOTS_ALL, PS, PS), jnp.float32) ** block_scale(part_keys[3], (SLOTS_ALL, PS, PS), ((0, 16),), -0.2, 0.2), 0.0, 2.0)
    positions = draw_positions(jax.random.fold_in(jax.random.fold_in(streams_of[6], part), 71), part)
    counts = draw_counts(jax.random.fold_in(jax.random.fold_in(streams_of[6], part), 71), part)
    return {"tile_object": tile_object, "probe_wave": probe_wave, "propagator_phase": propagator_phase, "diffraction": diffraction, "positions": positions, "counts": counts}


def exit_loss(patches, probe_wave, propagator_phase, pattern):
    wavefield = lax.complex(probe_wave[0], probe_wave[1])
    kernel = lax.complex(jnp.cos(propagator_phase), jnp.sin(propagator_phase))
    for layer_index in range(NS):
        wavefield = wavefield * lax.complex(patches[layer_index, 0], patches[layer_index, 1])
        if layer_index + 1 < NS:
            spectrum = jnp.fft.fft2(wavefield, norm='ortho')
            wavefield = jnp.fft.ifft2(kernel * spectrum, norm='ortho')
    farfield = jnp.fft.fft2(wavefield, norm='ortho')
    intensity = jnp.real(farfield) ** 2 + jnp.imag(farfield) ** 2
    return jnp.sum((intensity - pattern) ** 2)

def reference(tile_object, probe_wave, propagator_phase, diffraction, positions, counts):
    padded = jnp.concatenate([tile_object, tile_object[:, :, :PS]], axis=2)
    patch_gradient = jax.grad(exit_loss)
    anchor = jnp.zeros((), jnp.int32)

    def accumulate(summed, slot_number):
        holder = slot_number // SLOTS
        is_live = (slot_number % SLOTS < counts[holder]).astype(summed.dtype)
        row_start = (holder * TR + positions[slot_number, 0]).astype(jnp.int32)
        col_start = positions[slot_number, 1].astype(jnp.int32)
        corner = (anchor, anchor, row_start, col_start)
        patches = lax.dynamic_slice(padded, corner, (NS, 2, PS, PS))
        gradient = patch_gradient(patches, probe_wave, propagator_phase, diffraction[slot_number]) * is_live
        current = lax.dynamic_slice(summed, corner, (NS, 2, PS, PS))
        return (lax.dynamic_update_slice(summed, current + gradient, corner), None)
    summed, unused = lax.scan(accumulate, jnp.zeros_like(padded), jnp.arange(SLOTS_ALL, dtype=jnp.int32))
    top_rows = summed[:, :, :PS] + summed[:, :, OROWS:]
    return jnp.concatenate([top_rows, summed[:, :, PS:OROWS]], axis=2)
```

```python
import functools

import jax
import jax.numpy as jnp
import numpy as np
from jax import lax
from jax.experimental import pallas as pl
from jax.experimental.pallas import tpu as pltpu
from jax.sharding import PartitionSpec as P

PS = 128
NS = 4
SUB = 8
RC = PS // SUB
ITEMS = 3
CHUNKS = 20
BF = jnp.bfloat16
F32 = jnp.float32
I32 = jnp.int32
VMEM = pl.BlockSpec(memory_space=pltpu.VMEM)
SMEM = pl.BlockSpec(memory_space=pltpu.SMEM)
MESH = pl.DeviceIdType.MESH


def dft_parts():
    k = np.arange(PS)
    ang = (np.outer(k, k) % PS) * (2.0 * np.pi / PS)
    c = np.cos(ang) / np.sqrt(PS)
    s = -np.sin(ang) / np.sqrt(PS)
    forward = np.block([[c, s], [-s, c]]).astype(np.float32)
    inverse = np.block([[c, -s], [s, c]]).astype(np.float32)
    parts = []
    for m in (forward, inverse):
        hi = m.astype(BF)
        lo = (m - hi.astype(np.float32)).astype(BF)
        parts += [hi, lo]
    return np.stack(parts)


def pick(flag, a, b):
    return {k: jnp.where(flag, a[k], b[k]) for k in a}


def assign(meta):
    slots = 4
    rows = [meta[i, 0] for i in range(slots)]
    cols = [meta[i, 1] for i in range(slots)]
    count = meta[slots, 0]
    key = [jnp.where(i < count, rows[i], 1000) for i in range(slots)]
    rank = []
    for i in range(slots):
        r = jnp.int32(0)
        for j in range(slots):
            if j != i:
                ahead = key[j] <= key[i] if j < i else key[j] < key[i]
                r = r + jnp.where(ahead, 1, 0)
        rank.append(r)

    def ordered(vals):
        out = []
        for r in range(slots):
            v = jnp.int32(0)
            for i in range(slots):
                v = v + jnp.where(rank[i] == r, vals[i], 0)
            out.append(v)
        return out

    row, col, slot = ordered(rows), ordered(cols), ordered([jnp.int32(i) for i in range(slots)])
    above = [(row[r] + (SUB - 1)) >> 3 for r in range(slots)]
    below = [jnp.where(r < count, RC - (row[r] >> 3), 0) for r in range(slots)]
    best, cut = jnp.int32(10000), jnp.int32(0)
    for k in range(ITEMS + 1):
        up = sum(above[:k], jnp.int32(0))
        down = sum(below[k:], jnp.int32(0))
        cost = jnp.maximum(up, down)
        bad = (k > count) | (count - k > ITEMS)
        cost = jnp.where(bad, 20000, cost)
        cut = jnp.where(cost < best, k, cut)
        best = jnp.minimum(cost, best)

    def listed(first, end, sizes, upward):
        items, off = [], jnp.int32(0)
        for u in range(ITEMS):
            at = first + u
            live = at < end

            def take(vals):
                v = jnp.int32(0)
                for r in range(slots):
                    v = v + jnp.where(live & (at == r), vals[r], 0)
                return v

            n, c = take(sizes), take(col)
            items.append(
                dict(
                    live=jnp.where(live, 1, 0),
                    row=take(row),
                    block=c >> 7,
                    lane=c & (PS - 1),
                    slot=take(slot),
                    off=off,
                    n=n,
                    base=jnp.int32(0) if upward else RC - n,
                )
            )
            off = off + n
        return items

    return listed(jnp.int32(0), cut, above, True), listed(cut, count, below, False)


def listings(own_meta, prev_meta, even):
    up_own, down_own = assign(own_meta)
    up_prev, down_prev = assign(prev_meta)
    sends = [
        [pick(even, a, b) for a, b in zip(down_own, up_prev)],
        [pick(even, a, b) for a, b in zip(up_prev, down_own)],
    ]
    works = [
        [pick(even, a, b) for a, b in zip(up_own, down_prev)],
        [pick(even, a, b) for a, b in zip(down_prev, up_own)],
    ]
    return sends, works, down_own


def chunk_of(items, j):
    second, third = j >= items[1]["off"], j >= items[2]["off"]

    def get(k):
        return jnp.where(third, items[2][k], jnp.where(second, items[1][k], items[0][k]))

    r = jnp.clip(j - get("off") + get("base"), 0, RC - 1)
    return get, jnp.where(third, 2, jnp.where(second, 1, 0)), r


def split(x):
    hi = x.astype(BF)
    return hi, (x - hi.astype(F32)).astype(BF)


def dot(a, b):
    return jnp.dot(a, b, preferred_element_type=F32)


def grad_kernel(
    own_meta, prev_meta, tile_ref, first_ref, kre_ref, kim_ref, diff_ref, tab_ref,
    mine_ref, theirs_ref,
    pack_ref, got_ref, stage_ref, dpack_ref, dgot_ref, w_ref, t_ref, g_ref, gpack_ref, tile_b,
    fs, fr, ds, dr, gs_sem, gr_sem,
):
    me, n = lax.axis_index("ty"), lax.axis_size("ty")
    following, previous = lax.rem(me + 1, n), lax.rem(me + n - 1, n)
    even = lax.rem(me, 2) == 0
    peers = [jnp.where(even, following, previous), jnp.where(even, previous, following)]

    barrier = pltpu.get_barrier_semaphore()
    for peer in peers:
        pl.semaphore_signal(barrier, inc=1, device_id={"ty": peer}, device_id_type=MESH)

    sends, works, down_own = listings(own_meta, prev_meta, even)
    upward = [even, jnp.logical_not(even)]
    last = tile_ref.shape[3] // PS - 1
    row = lax.broadcasted_iota(I32, (PS, PS), 0)
    lane = lax.broadcasted_iota(I32, (PS, PS), 1)
    lane8 = lax.broadcasted_iota(I32, (SUB, PS), 1)

    def columns(block):
        return block, jnp.minimum(block + 1, last)

    for k in range(last + 1):
        for s in range(NS):
            for b in range(2):
                wide = tile_ref[s, b, :, k * PS : (k + 1) * PS]
                tile_b[k, s, b] = wide.reshape(RC, SUB, PS)

    def fetch(g, s):
        return pltpu.make_async_remote_copy(
            src_ref=pack_ref.at[g, s],
            dst_ref=got_ref.at[g, s],
            send_sem=fs.at[g, s],
            recv_sem=fr.at[g, s],
            device_id={"ty": peers[g]},
            device_id_type=MESH,
        )

    def give(g, s):
        return pltpu.make_async_remote_copy(
            src_ref=gpack_ref.at[g, s],
            dst_ref=theirs_ref.at[g, s],
            send_sem=gs_sem.at[g, s],
            recv_sem=gr_sem.at[g, s],
            device_id={"ty": peers[g]},
            device_id_type=MESH,
        )

    patterns = pltpu.make_async_remote_copy(
        src_ref=dpack_ref,
        dst_ref=dgot_ref,
        send_sem=ds.at[0],
        recv_sem=dr.at[0],
        device_id={"ty": following},
        device_id_type=MESH,
    )

    pl.semaphore_wait(barrier, 2)

    tables = []
    for g in range(2):
        table = []
        for j in range(CHUNKS):
            get, _, r = chunk_of(sends[g], j)
            here, after = columns(get("block"))
            table.append((here, after, get("lane"), r))
        tables.append(table)
    for s in range(NS):
        for g in (1, 0):
            for j, (here, after, shift, rows) in enumerate(tables[g]):
                for b in range(2):
                    pack_ref[g, s, j, b] = jnp.where(
                        lane8 >= shift, tile_b[here, s, b, rows], tile_b[after, s, b, rows]
                    )
            fetch(g, s).start()
    for u in range(ITEMS):
        dpack_ref[u] = diff_ref[down_own[u]["slot"]]
    patterns.start()

    def left(z, inv):
        hi, lo = tab_ref[2 - 2 * inv], tab_ref[3 - 2 * inv]
        h, l = split(z)
        return dot(hi, h) + dot(hi, l) + dot(lo, h)

    def right(z, inv):
        hi, lo = tab_ref[2 * inv], tab_ref[2 * inv + 1]
        h, l = split(z)
        return dot(h, hi) + dot(l, hi) + dot(h, lo)

    def tall(zs):
        return jnp.concatenate([jnp.concatenate(z, axis=0) for z in zs], axis=1)

    def untall(y):
        return [(y[:PS, i * PS : (i + 1) * PS], y[PS:, i * PS : (i + 1) * PS]) for i in range(ITEMS)]

    def wide(zs):
        return jnp.concatenate([jnp.concatenate(z, axis=1) for z in zs], axis=0)

    def unwide(y):
        return [(y[i * PS : (i + 1) * PS, :PS], y[i * PS : (i + 1) * PS, PS:]) for i in range(ITEMS)]

    def forward(zs):
        return unwide(right(wide(untall(left(tall(zs), 0))), 0))

    def backward(zs):
        return untall(left(tall(unwide(right(wide(zs), 1))), 1))

    def kernel_product(z, sign):
        re, im = z
        kre, kim = kre_ref[...], kim_ref[...] * sign
        return re * kre - im * kim, re * kim + im * kre

    def work(g):
        items, ups = works[g], upward[g]
        signed = row * jnp.where(ups, 1, -1)

        def ours(item):
            return signed >= jnp.where(ups, item["row"], 1 - item["row"])

        def object_of(s):
            stage_ref[pl.ds(RC, CHUNKS)] = got_ref[g, s]
            for u, item in enumerate(items):
                here, after = columns(item["block"])
                start = RC + item["off"] - item["base"]
                mine = ours(item)
                for b in range(2):
                    own = jnp.where(
                        lane >= item["lane"],
                        tile_b[here, s, b].reshape(PS, PS),
                        tile_b[after, s, b].reshape(PS, PS),
                    )
                    got = jnp.concatenate([stage_ref[start + r, b] for r in range(RC)], axis=0)
                    t_ref[s, u, b] = jnp.where(mine, own, got)

        def through(s):
            zs = []
            for u in range(ITEMS):
                wre, wim, tre, tim = w_ref[s, u, 0], w_ref[s, u, 1], t_ref[s, u, 0], t_ref[s, u, 1]
                zs.append((wre * tre - wim * tim, wre * tim + wim * tre))
            return zs

        for u, item in enumerate(items):
            for b in range(2):
                w_ref[0, u, b] = first_ref[g, u, b]

        def advance(s, carry):
            fetch(g, s).wait_recv()
            object_of(s)
            zs = [kernel_product(z, 1.0) for z in forward(through(s))]
            for u, z in enumerate(backward(zs)):
                w_ref[s + 1, u, 0], w_ref[s + 1, u, 1] = z
            return carry

        lax.fori_loop(0, NS - 1, advance, 0)
        fetch(g, NS - 1).wait_recv()
        object_of(NS - 1)
        far = forward(through(NS - 1))
        if g == 0:
            patterns.wait_recv()
        grads = []
        for u, (re, im) in enumerate(far):
            item = items[u]
            pattern = jnp.where(ups, diff_ref[item["slot"]], dgot_ref[u])
            live = jnp.where(item["live"] > 0, 4.0, 0.0).astype(F32)
            f = (re * re + im * im - pattern) * live
            grads.append((re * f, im * f))
        grads = backward(grads)
        places = []
        for j in range(CHUNKS):
            _, which, r = chunk_of(items, j)
            places.append((which, r))

        def deposit(s, grads):
            for u, (gre, gim) in enumerate(grads):
                item = items[u]
                mine = ours(item)
                wre, wim = w_ref[s, u, 0], w_ref[s, u, 1]
                for b, val in enumerate((wre * gre + wim * gim, wre * gim - wim * gre)):
                    mine_ref[g, u, s, b] = jnp.where(mine, val, 0.0)
                    g_ref[u, b] = jnp.where(mine, 0.0, val).reshape(RC, SUB, PS)
            for j, (which, r) in enumerate(places):
                for b in range(2):
                    gpack_ref[g, s, j, b] = g_ref[which, b, r]
            give(g, s).start()

        def retreat(i, grads):
            s = NS - 1 - i
            deposit(s, grads)
            zs = []
            for u, (gre, gim) in enumerate(grads):
                tre, tim = t_ref[s, u, 0], t_ref[s, u, 1]
                zs.append((gre * tre + gim * tim, gim * tre - gre * tim))
            return tuple(backward([kernel_product(z, -1.0) for z in forward(zs)]))

        grads = lax.fori_loop(0, NS - 1, retreat, tuple(grads))
        deposit(0, grads)

    for g in range(2):
        work(g)
    for g in range(2):
        for s in range(NS):
            fetch(g, s).wait_send()
            give(g, s).wait_send()
    patterns.wait_send()
    for g in range(2):
        for s in range(NS):
            give(g, s).wait_recv()


def first_kernel(own_meta, prev_meta, even_ref, probe_ref, out_ref):
    _, works, _ = listings(own_meta, prev_meta, even_ref[0] == 1)
    for g in range(2):
        for u, item in enumerate(works[g]):
            for b in range(2):
                out_ref[g, u, b] = pltpu.roll(pltpu.roll(probe_ref[b], item["row"], 0), item["lane"], 1)


def first_waves(own_meta, prev_meta, even, probe):
    return pl.pallas_call(
        first_kernel,
        out_shape=jax.ShapeDtypeStruct((2, ITEMS, 2, PS, PS), F32),
        in_specs=[SMEM] * 3 + [VMEM],
        out_specs=VMEM,
        compiler_params=pltpu.CompilerParams(vmem_limit_bytes=8 << 20),
        cost_estimate=pl.CostEstimate(flops=10**3, bytes_accessed=10**4, transcendentals=0),
    )(own_meta, prev_meta, even, probe)


def gradients(own_meta, prev_meta, tile, first, kre, kim, diff):
    tables = jnp.asarray(dft_parts())
    packed = (2, NS, CHUNKS, 2, SUB, PS)
    dma = pltpu.SemaphoreType.DMA
    return pl.pallas_call(
        grad_kernel,
        out_shape=(
            jax.ShapeDtypeStruct((2, ITEMS, NS, 2, PS, PS), F32),
            jax.ShapeDtypeStruct(packed, F32),
        ),
        in_specs=[SMEM] * 2 + [VMEM] * 6,
        out_specs=(VMEM, VMEM),
        scratch_shapes=[
            pltpu.VMEM(packed, F32),
            pltpu.VMEM(packed, F32),
            pltpu.VMEM((CHUNKS + 2 * RC, 2, SUB, PS), F32),
            pltpu.VMEM((ITEMS, PS, PS), F32),
            pltpu.VMEM((ITEMS, PS, PS), F32),
            pltpu.VMEM((NS, ITEMS, 2, PS, PS), F32),
            pltpu.VMEM((NS, ITEMS, 2, PS, PS), F32),
            pltpu.VMEM((ITEMS, 2, RC, SUB, PS), F32),
            pltpu.VMEM(packed, F32),
            pltpu.VMEM((tile.shape[3] // PS, NS, 2, RC, SUB, PS), F32),
            dma((2, NS)),
            dma((2, NS)),
            dma((1,)),
            dma((1,)),
            dma((2, NS)),
            dma((2, NS)),
        ],
        compiler_params=pltpu.CompilerParams(
            collective_id=0, has_side_effects=True, vmem_limit_bytes=32 << 20
        ),
        cost_estimate=pl.CostEstimate(flops=8 * 10**9, bytes_accessed=5 * 10**6, transcendentals=0),
    )(own_meta, prev_meta, tile, first, kre, kim, diff, tables)


def place_kernel(own_meta, prev_meta, even_ref, mine_ref, theirs_ref, out_ref):
    even = even_ref[0] == 1
    sends, works, _ = listings(own_meta, prev_meta, even)
    last = out_ref.shape[3] // PS - 1
    lane = lax.broadcasted_iota(I32, (PS, PS), 1)
    lane8 = lax.broadcasted_iota(I32, (SUB, PS), 1)
    out_ref[...] = jnp.zeros_like(out_ref)

    def columns(block):
        here = pl.ds(pl.multiple_of(block * PS, PS), PS)
        after = pl.ds(pl.multiple_of(jnp.minimum(block + 1, last) * PS, PS), PS)
        return here, after

    for g in range(2):
        for u in range(ITEMS):
            item = works[g][u]
            here, after = columns(item["block"])

            @pl.when(item["live"] > 0)
            def _():
                for b in range(2):
                    val = mine_ref[g, u, 0, b]
                    out_ref[0, b, :, here] += jnp.where(lane >= item["lane"], val, 0.0)
                    out_ref[0, b, :, after] += jnp.where(lane >= item["lane"], 0.0, val)

            sent = sends[g][u]
            shere, safter = columns(sent["block"])

            def add(i, carry):
                rows = pl.ds(pl.multiple_of((sent["base"] + i) * SUB, SUB), SUB)
                for b in range(2):
                    val = theirs_ref[g, 0, sent["off"] + i, b]
                    out_ref[0, b, rows, shere] += jnp.where(lane8 >= sent["lane"], val, 0.0)
                    out_ref[0, b, rows, safter] += jnp.where(lane8 >= sent["lane"], 0.0, val)
                return carry

            lax.fori_loop(0, sent["n"], add, 0)


def place(own_meta, prev_meta, even, mine, theirs, width):
    return pl.pallas_call(
        place_kernel,
        grid_spec=pltpu.PrefetchScalarGridSpec(
            num_scalar_prefetch=3,
            grid=(NS,),
            in_specs=[
                pl.BlockSpec((2, ITEMS, 1, 2, PS, PS), lambda a, *_: (0, 0, a, 0, 0, 0)),
                pl.BlockSpec((2, 1, CHUNKS, 2, SUB, PS), lambda a, *_: (0, a, 0, 0, 0, 0)),
            ],
            out_specs=pl.BlockSpec((1, 2, PS, width), lambda a, *_: (a, 0, 0, 0)),
        ),
        out_shape=jax.ShapeDtypeStruct((NS, 2, PS, width), F32),
        compiler_params=pltpu.CompilerParams(vmem_limit_bytes=16 << 20),
        cost_estimate=pl.CostEstimate(flops=10**6, bytes_accessed=7 * 10**6, transcendentals=0),
    )(own_meta, prev_meta, even, mine, theirs)


def per_device(tile_object, probe_wave, propagator_phase, diffraction, positions, counts):
    width = tile_object.shape[3]
    peers = lax.axis_size("ty")
    own_meta = jnp.concatenate([positions, jnp.stack([counts, counts], axis=1)], axis=0)
    prev_meta = lax.ppermute(own_meta, "ty", [(i, (i + 1) % peers) for i in range(peers)])
    kre, kim = jnp.cos(propagator_phase), jnp.sin(propagator_phase)
    even = jnp.where(lax.axis_index("ty") % 2 == 0, 1, 0).astype(I32).reshape(1)
    first = first_waves(own_meta, prev_meta, even, probe_wave)
    mine, theirs = gradients(own_meta, prev_meta, tile_object, first, kre, kim, diffraction)
    return place(own_meta, prev_meta, even, mine, theirs, width)


def solution(mesh):
    in_specs = (
        P(None, None, ("grp", "ty"), None),
        P(),
        P(),
        P(("grp", "ty"), None, None),
        P(("grp", "ty"), None),
        P(("grp", "ty")),
    )
    out_specs = P(None, None, ("grp", "ty"), None)
    return jax.shard_map(
        per_device, mesh=mesh, in_specs=in_specs, out_specs=out_specs, check_vma=False
    )
```

```python
import functools

import jax
import jax.numpy as jnp
import numpy as np
from jax import lax
from jax.experimental import pallas as pl
from jax.experimental.pallas import tpu as pltpu
from jax.sharding import PartitionSpec as P

PS = 128
NS = 4
SUB = 8
RC = PS // SUB
ITEMS = 3
CHUNKS = 20
BF = jnp.bfloat16
F32 = jnp.float32
I32 = jnp.int32
VMEM = pl.BlockSpec(memory_space=pltpu.VMEM)
SMEM = pl.BlockSpec(memory_space=pltpu.SMEM)
MESH = pl.DeviceIdType.MESH


def dft_parts():
    k = np.arange(PS)
    ang = (np.outer(k, k) % PS) * (2.0 * np.pi / PS)
    c = np.cos(ang) / np.sqrt(PS)
    s = -np.sin(ang) / np.sqrt(PS)
    forward = np.block([[c, s], [-s, c]]).astype(np.float32)
    inverse = np.block([[c, -s], [s, c]]).astype(np.float32)
    parts = []
    for m in (forward, inverse):
        hi = m.astype(BF)
        lo = (m - hi.astype(np.float32)).astype(BF)
        parts += [hi, lo]
    return np.stack(parts)


def pick(flag, a, b):
    return {k: jnp.where(flag, a[k], b[k]) for k in a}


def assign(rows, cols, count):
    slots = len(rows)
    key = [jnp.where(i < count, rows[i], 1000) for i in range(slots)]
    rank = []
    for i in range(slots):
        r = jnp.int32(0)
        for j in range(slots):
            if j != i:
                ahead = key[j] <= key[i] if j < i else key[j] < key[i]
                r = r + jnp.where(ahead, 1, 0)
        rank.append(r)

    def ordered(vals):
        out = []
        for r in range(slots):
            v = jnp.int32(0)
            for i in range(slots):
                v = v + jnp.where(rank[i] == r, vals[i], 0)
            out.append(v)
        return out

    row, col, slot = ordered(rows), ordered(cols), ordered([jnp.int32(i) for i in range(slots)])
    above = [(row[r] + (SUB - 1)) >> 3 for r in range(slots)]
    below = [jnp.where(r < count, RC - (row[r] >> 3), 0) for r in range(slots)]
    best, cut = jnp.int32(10000), jnp.int32(0)
    for k in range(ITEMS + 1):
        up = sum(above[:k], jnp.int32(0))
        down = sum(below[k:], jnp.int32(0))
        cost = jnp.maximum(up, down)
        bad = (k > count) | (count - k > ITEMS)
        cost = jnp.where(bad, 20000, cost)
        cut = jnp.where(cost < best, k, cut)
        best = jnp.minimum(cost, best)

    def listed(first, end, sizes, upward):
        items, off = [], jnp.int32(0)
        for u in range(ITEMS):
            at = first + u
            live = at < end

            def take(vals):
                v = jnp.int32(0)
                for r in range(slots):
                    v = v + jnp.where(live & (at == r), vals[r], 0)
                return v

            n, c = take(sizes), take(col)
            items.append(
                dict(
                    live=jnp.where(live, 1, 0),
                    row=take(row) if upward else jnp.where(live, take(row), PS),
                    block=c >> 7,
                    lane=c & (PS - 1),
                    slot=take(slot),
                    off=off,
                    n=n,
                    base=jnp.int32(0) if upward else RC - n,
                )
            )
            off = off + n
        return items

    return listed(jnp.int32(0), cut, above, True), listed(cut, count, below, False)


def told_slots(ref, slots):
    rows = [ref[0, i] for i in range(slots)]
    return rows, [ref[0, slots + i] for i in range(slots)], ref[0, 2 * slots]


def listings(own, prev, even):
    up_own, down_own = assign(*own)
    up_prev, down_prev = assign(*prev)
    sends = [
        [pick(even, a, b) for a, b in zip(down_own, up_prev)],
        [pick(even, a, b) for a, b in zip(up_prev, down_own)],
    ]
    works = [
        [pick(even, a, b) for a, b in zip(up_own, down_prev)],
        [pick(even, a, b) for a, b in zip(down_prev, up_own)],
    ]
    return sends, works, down_own


def chunk_of(items, j):
    second, third = j >= items[1]["off"], j >= items[2]["off"]

    def get(k):
        return jnp.where(third, items[2][k], jnp.where(second, items[1][k], items[0][k]))

    r = jnp.clip(j - get("off") + get("base"), 0, RC - 1)
    return get, jnp.where(third, 2, jnp.where(second, 1, 0)), r


def split(x):
    hi = x.astype(BF)
    return hi, (x - hi.astype(F32)).astype(BF)


def dot(a, b):
    return jnp.dot(a, b, preferred_element_type=F32)


def grad_kernel(
    count_ref, pos_hbm, tile_hbm, probe_hbm, phase_hbm, diff_hbm, tab_hbm,
    base_ref, theirs_ref, prev_ref, hello_ref,
    pos_ref, tile_ref, probe_ref, kre_ref, kim_ref, diff_ref, tab_ref,
    meta_ref, pack_ref, got_ref, stage_ref, dpack_ref, dgot_ref,
    w_ref, t_ref, g_ref, gpack_ref,
    ts, ls, hs, fs, fr, ds, dr, gs_sem, gr_sem,
):
    me, n = lax.axis_index("ty"), lax.axis_size("ty")
    following, previous = lax.rem(me + 1, n), lax.rem(me + n - 1, n)
    even = lax.rem(me, 2) == 0
    peers = [jnp.where(even, following, previous), jnp.where(even, previous, following)]
    slots = pos_ref.shape[1]
    blocks = tile_hbm.shape[4] // PS
    last = blocks - 1

    barrier = pltpu.get_barrier_semaphore()
    for peer in peers:
        pl.semaphore_signal(barrier, inc=1, device_id={"ty": peer}, device_id_type=MESH)

    def tile_copy(s, k):
        return pltpu.make_async_copy(
            tile_hbm.at[s, :, :, :, pl.ds(k * PS, PS)], tile_ref.at[k, s], ts.at[s, k]
        )

    loads = [
        pltpu.make_async_copy(probe_hbm, probe_ref, ls.at[0]),
        pltpu.make_async_copy(phase_hbm, kre_ref, ls.at[1]),
        pltpu.make_async_copy(tab_hbm, tab_ref, ls.at[2]),
        pltpu.make_async_copy(diff_hbm, diff_ref, ls.at[3]),
    ]
    own = pltpu.make_async_copy(pos_hbm, pos_ref, hs.at[3])
    own.start()
    for s in range(NS):
        for k in range(blocks):
            tile_copy(s, k).start()
    for copy in loads:
        copy.start()
    own.wait()

    at = lax.broadcasted_iota(I32, (SUB, PS), 1)
    told = jnp.where(at == 2 * slots, count_ref[0], 0)
    for i in range(slots):
        told = jnp.where(at == i, pos_ref[0, i], told)
        told = jnp.where(at == slots + i, pos_ref[1, i], told)
    hello_ref[...] = told
    pl.semaphore_wait(barrier, 2)
    hello = pltpu.make_async_remote_copy(
        src_ref=hello_ref,
        dst_ref=prev_ref,
        send_sem=hs.at[0],
        recv_sem=hs.at[1],
        device_id={"ty": following},
        device_id_type=MESH,
    )
    hello.start()
    hello.wait()
    learn = pltpu.make_async_copy(prev_ref, meta_ref, hs.at[2])
    learn.start()
    learn.wait()

    own_slots = (
        [pos_ref[0, i] for i in range(slots)], [pos_ref[1, i] for i in range(slots)], count_ref[0]
    )
    sends, works, down_own = listings(own_slots, told_slots(meta_ref, slots), even)
    upward = [even, jnp.logical_not(even)]
    row = lax.broadcasted_iota(I32, (PS, PS), 0)
    lane = lax.broadcasted_iota(I32, (PS, PS), 1)
    lane8 = lax.broadcasted_iota(I32, (SUB, PS), 1)

    def fetch(g, s):
        return pltpu.make_async_remote_copy(
            src_ref=pack_ref.at[g, s],
            dst_ref=got_ref.at[g, s],
            send_sem=fs.at[g, s],
            recv_sem=fr.at[g, s],
            device_id={"ty": peers[g]},
            device_id_type=MESH,
        )

    def give(g, s):
        return pltpu.make_async_remote_copy(
            src_ref=gpack_ref.at[g, s],
            dst_ref=theirs_ref.at[g, s],
            send_sem=gs_sem.at[g, s],
            recv_sem=gr_sem.at[g, s],
            device_id={"ty": peers[g]},
            device_id_type=MESH,
        )

    patterns = pltpu.make_async_remote_copy(
        src_ref=dpack_ref,
        dst_ref=dgot_ref,
        send_sem=ds.at[0],
        recv_sem=dr.at[0],
        device_id={"ty": following},
        device_id_type=MESH,
    )

    tables = []
    for g in range(2):
        table = []
        for j in range(CHUNKS):
            get, _, r = chunk_of(sends[g], j)
            block = get("block")
            table.append((block, jnp.minimum(block + 1, last), get("lane"), r))
        tables.append(table)
    for s in range(NS):
        for k in range(blocks):
            tile_copy(s, k).wait()
    for s in range(NS):
        for g in (1, 0):
            for j, (here, after, shift, r) in enumerate(tables[g]):
                for b in range(2):
                    pack_ref[g, s, j, b] = jnp.where(
                        lane8 >= shift, tile_ref[here, s, b, r], tile_ref[after, s, b, r]
                    )
            fetch(g, s).start()
    for copy in loads:
        copy.wait()
    for u in range(ITEMS):
        dpack_ref[u] = diff_ref[down_own[u]["slot"]]
    patterns.start()
    phase = kre_ref[...]
    kre_ref[...] = jnp.cos(phase)
    kim_ref[...] = jnp.sin(phase)

    def left(zs, inv):
        hi, lo = tab_ref[2 - 2 * inv], tab_ref[3 - 2 * inv]
        out = []
        for z in zs:
            h, l = split(jnp.concatenate(z, axis=0))
            y = dot(hi, jnp.concatenate([h, l], axis=1))
            y = y[:, :PS] + y[:, PS:] + dot(lo, h)
            out.append((y[:PS], y[PS:]))
        return out

    def right(zs, inv):
        hi, lo = tab_ref[2 * inv], tab_ref[2 * inv + 1]
        out = []
        for z in zs:
            h, l = split(jnp.concatenate(z, axis=1))
            y = dot(h, hi) + dot(l, hi) + dot(h, lo)
            out.append((y[:, :PS], y[:, PS:]))
        return out

    def forward(zs):
        return right(left(zs, 0), 0)

    def backward(zs):
        return left(right(zs, 1), 1)

    def kernel_product(z, sign):
        re, im = z
        kre, kim = kre_ref[...], kim_ref[...] * sign
        return re * kre - im * kim, re * kim + im * kre

    def work(g):
        items, ups = works[g], upward[g]
        signed = row * jnp.where(ups, 1, -1)
        target = [
            jnp.where(lane8 >= item["lane"], item["block"], item["block"] + 1) for item in items
        ]

        def ours(item):
            return signed >= jnp.where(ups, item["row"], 1 - item["row"])

        def object_of(s):
            stage_ref[pl.ds(RC, CHUNKS)] = got_ref[g, s]
            for u, item in enumerate(items):
                here, after = item["block"], jnp.minimum(item["block"] + 1, last)
                start = RC + item["off"] - item["base"]
                mine = ours(item)
                for b in range(2):
                    own = jnp.where(
                        lane >= item["lane"],
                        tile_ref[here, s, b].reshape(PS, PS),
                        tile_ref[after, s, b].reshape(PS, PS),
                    )
                    got = jnp.concatenate([stage_ref[start + r, b] for r in range(RC)], axis=0)
                    t_ref[s, u, b] = jnp.where(mine, own, got)

        def through(s):
            zs = []
            for u in range(ITEMS):
                wre, wim, tre, tim = w_ref[s, u, 0], w_ref[s, u, 1], t_ref[s, u, 0], t_ref[s, u, 1]
                zs.append((wre * tre - wim * tim, wre * tim + wim * tre))
            return zs

        for u, item in enumerate(items):
            down = item["row"] & (PS - 1)
            for b in range(2):
                w_ref[0, u, b] = pltpu.roll(pltpu.roll(probe_ref[b], down, 0), item["lane"], 1)

        def advance(s, carry):
            fetch(g, s).wait_recv()
            object_of(s)
            zs = [kernel_product(z, 1.0) for z in forward(through(s))]
            for u, z in enumerate(backward(zs)):
                w_ref[s + 1, u, 0], w_ref[s + 1, u, 1] = z
            return carry

        lax.fori_loop(0, NS - 1, advance, 0)
        fetch(g, NS - 1).wait_recv()
        object_of(NS - 1)
        far = forward(through(NS - 1))
        if g == 0:
            patterns.wait_recv()
        grads = []
        for u, (re, im) in enumerate(far):
            item = items[u]
            pattern = jnp.where(ups, diff_ref[item["slot"]], dgot_ref[u])
            live = jnp.where(item["live"] > 0, 4.0, 0.0).astype(F32)
            f = (re * re + im * im - pattern) * live
            grads.append((re * f, im * f))
        grads = backward(grads)
        places = []
        for j in range(CHUNKS):
            _, which, r = chunk_of(items, j)
            places.append((which, r))

        def deposit(s, grads):
            mines = []
            for u, (gre, gim) in enumerate(grads):
                mine = ours(items[u])
                wre, wim = w_ref[s, u, 0], w_ref[s, u, 1]
                both = []
                for b, val in enumerate((wre * gre + wim * gim, wre * gim - wim * gre)):
                    both.append(jnp.where(mine, val, 0.0).reshape(RC, SUB, PS))
                    g_ref[u, b] = jnp.where(mine, 0.0, val).reshape(RC, SUB, PS)
                mines.append(both)
            for j, (which, r) in enumerate(places):
                for b in range(2):
                    gpack_ref[g, s, j, b] = g_ref[which, b, r]
            give(g, s).start()
            for k in range(blocks):
                at_k = [(t == k)[None] for t in target]
                for b in range(2):
                    add = sum(jnp.where(m, v[b], 0.0) for m, v in zip(at_k, mines))
                    if g == 0:
                        base_ref[k, s, b] = add
                    else:
                        base_ref[k, s, b] += add

        def retreat(i, grads):
            s = NS - 1 - i
            deposit(s, grads)
            zs = []
            for u, (gre, gim) in enumerate(grads):
                tre, tim = t_ref[s, u, 0], t_ref[s, u, 1]
                zs.append((gre * tre + gim * tim, gim * tre - gre * tim))
            return tuple(backward([kernel_product(z, -1.0) for z in forward(zs)]))

        grads = lax.fori_loop(0, NS - 1, retreat, tuple(grads))
        deposit(0, grads)

    for g in range(2):
        work(g)
    for g in range(2):
        for s in range(NS):
            fetch(g, s).wait_send()
            give(g, s).wait_send()
    patterns.wait_send()
    for g in range(2):
        for s in range(NS):
            give(g, s).wait_recv()


def gradients(pos, count, tile, probe, phase, diff):
    tables = jnp.asarray(dft_parts())
    operands = [
        pltpu.with_memory_space_constraint(x, pltpu.HBM)
        for x in (pos, tile, probe, phase, diff, tables)
    ]
    blocks = tile.shape[4] // PS
    packed = (2, NS, CHUNKS, 2, SUB, PS)
    halves = (blocks, NS, 2, RC, SUB, PS)
    dma = pltpu.SemaphoreType.DMA
    return pl.pallas_call(
        grad_kernel,
        out_shape=(
            jax.ShapeDtypeStruct(halves, F32),
            jax.ShapeDtypeStruct(packed, F32),
            jax.ShapeDtypeStruct((SUB, PS), I32),
            jax.ShapeDtypeStruct((SUB, PS), I32),
        ),
        in_specs=[SMEM] + [pl.BlockSpec(memory_space=pltpu.HBM)] * len(operands),
        out_specs=(VMEM,) * 4,
        scratch_shapes=[
            pltpu.SMEM(pos.shape, I32),
            pltpu.VMEM(halves, F32),
            pltpu.VMEM((2, PS, PS), F32),
            pltpu.VMEM((PS, PS), F32),
            pltpu.VMEM((PS, PS), F32),
            pltpu.VMEM(diff.shape, F32),
            pltpu.VMEM(tables.shape, BF),
            pltpu.SMEM((SUB, PS), I32),
            pltpu.VMEM(packed, F32),
            pltpu.VMEM(packed, F32),
            pltpu.VMEM((CHUNKS + 2 * RC, 2, SUB, PS), F32),
            pltpu.VMEM((ITEMS, PS, PS), F32),
            pltpu.VMEM((ITEMS, PS, PS), F32),
            pltpu.VMEM((NS, ITEMS, 2, PS, PS), F32),
            pltpu.VMEM((NS, ITEMS, 2, PS, PS), F32),
            pltpu.VMEM((ITEMS, 2, RC, SUB, PS), F32),
            pltpu.VMEM(packed, F32),
            dma((NS, blocks)),
            dma((4,)),
            dma((4,)),
            dma((2, NS)),
            dma((2, NS)),
            dma((1,)),
            dma((1,)),
            dma((2, NS)),
            dma((2, NS)),
        ],
        compiler_params=pltpu.CompilerParams(
            collective_id=0, has_side_effects=True, vmem_limit_bytes=40 << 20
        ),
        cost_estimate=pl.CostEstimate(flops=8 * 10**9, bytes_accessed=5 * 10**6, transcendentals=0),
    )(count, *operands)


def place_kernel(slots, prev_ref, own_ref, base_ref, theirs_ref, out_hbm, sum_ref, prev_s, own_s, sems):
    even = lax.rem(lax.axis_index("ty"), 2) == 0
    learn = [
        pltpu.make_async_copy(prev_ref, prev_s, sems.at[NS]),
        pltpu.make_async_copy(own_ref, own_s, sems.at[NS + 1]),
    ]
    for copy in learn:
        copy.start()
    for copy in learn:
        copy.wait()
    sends, _, _ = listings(told_slots(own_s, slots), told_slots(prev_s, slots), even)
    blocks = base_ref.shape[0]
    lane8 = lax.broadcasted_iota(I32, (SUB, PS), 1)
    copies = []
    for s in range(NS):
        for k in range(blocks):
            for b in range(2):
                sum_ref[s, b, :, :, k * PS : (k + 1) * PS] = base_ref[k, s, b]
        for g in range(2):
            for item in sends[g]:
                block = item["block"]
                here = pl.ds(pl.multiple_of(block * PS, PS), PS)
                after = pl.ds(pl.multiple_of(jnp.minimum(block + 1, blocks - 1) * PS, PS), PS)

                def add(i, carry):
                    r, j = item["base"] + i, item["off"] + i
                    got = [theirs_ref[g, s, j, b] for b in range(2)]
                    old = [(sum_ref[s, b, r, :, here]) for b in range(2)]
                    for b in range(2):
                        sum_ref[s, b, r, :, here] = old[b] + jnp.where(lane8 >= item["lane"], got[b], 0.0)
                    old = [(sum_ref[s, b, r, :, after]) for b in range(2)]
                    for b in range(2):
                        sum_ref[s, b, r, :, after] = old[b] + jnp.where(lane8 >= item["lane"], 0.0, got[b])
                    return carry

                lax.fori_loop(0, item["n"], add, 0)
        copy = pltpu.make_async_copy(sum_ref.at[s], out_hbm.at[s], sems.at[s])
        copy.start()
        copies.append(copy)
    for copy in copies:
        copy.wait()


def place(slots, prev, own, base, theirs):
    shape = (NS, 2, RC, SUB, base.shape[0] * PS)
    return pl.pallas_call(
        functools.partial(place_kernel, slots),
        in_specs=[VMEM] * 4,
        out_specs=pl.BlockSpec(memory_space=pltpu.HBM),
        out_shape=jax.ShapeDtypeStruct(shape, F32),
        scratch_shapes=[
            pltpu.VMEM(shape, F32),
            pltpu.SMEM((SUB, PS), I32),
            pltpu.SMEM((SUB, PS), I32),
            pltpu.SemaphoreType.DMA((NS + 2,)),
        ],
        compiler_params=pltpu.CompilerParams(vmem_limit_bytes=16 << 20),
        cost_estimate=pl.CostEstimate(flops=10**6, bytes_accessed=7 * 10**6, transcendentals=0),
    )(prev, own, base, theirs)


def per_device(tile_object, probe_wave, propagator_phase, diffraction, positions, counts):
    width = tile_object.shape[3]
    pos = positions.T
    tile = tile_object.reshape(NS, 2, RC, SUB, width)
    base, theirs, prev, own = gradients(pos, counts, tile, probe_wave, propagator_phase, diffraction)
    return place(positions.shape[0], prev, own, base, theirs).reshape(tile_object.shape)


def solution(mesh):
    in_specs = (
        P(None, None, ("grp", "ty"), None),
        P(),
        P(),
        P(("grp", "ty"), None, None),
        P(("grp", "ty"), None),
        P(("grp", "ty")),
    )
    out_specs = P(None, None, ("grp", "ty"), None)
    return jax.shard_map(
        per_device, mesh=mesh, in_specs=in_specs, out_specs=out_specs, check_vma=False
    )
```

```python
import functools

import jax
import jax.numpy as jnp
import numpy as np
from jax import lax
from jax.experimental import pallas as pl
from jax.experimental.pallas import tpu as pltpu
from jax.sharding import PartitionSpec as P

PS = 128
NS = 4
SUB = 8
RC = PS // SUB
ITEMS = (2, 3)
SHORT = 2 * RC
LONG = 20
BF = jnp.bfloat16
F32 = jnp.float32
I32 = jnp.int32
VMEM = pl.BlockSpec(memory_space=pltpu.VMEM)
SMEM = pl.BlockSpec(memory_space=pltpu.SMEM)
MESH = pl.DeviceIdType.MESH


def dft_parts():
    k = np.arange(PS)
    ang = (np.outer(k, k) % PS) * (2.0 * np.pi / PS)
    c = np.cos(ang) / np.sqrt(PS)
    s = -np.sin(ang) / np.sqrt(PS)
    forward = np.block([[c, s], [-s, c]]).astype(np.float32)
    inverse = np.block([[c, -s], [s, c]]).astype(np.float32)
    parts = []
    for m in (forward, inverse):
        hi = m.astype(BF)
        lo = (m - hi.astype(np.float32)).astype(BF)
        parts += [hi, lo]
    return np.stack(parts)


def pick(flag, a, b):
    return {k: jnp.where(flag, a[k], b[k]) for k in a}


def assign(rows, cols, count, even):
    most = jnp.where(even, ITEMS[0], ITEMS[1])
    slots = len(rows)
    key = [jnp.where(i < count, rows[i], 1000) for i in range(slots)]
    rank = []
    for i in range(slots):
        r = jnp.int32(0)
        for j in range(slots):
            if j != i:
                ahead = key[j] <= key[i] if j < i else key[j] < key[i]
                r = r + jnp.where(ahead, 1, 0)
        rank.append(r)

    def ordered(vals):
        out = []
        for r in range(slots):
            v = jnp.int32(0)
            for i in range(slots):
                v = v + jnp.where(rank[i] == r, vals[i], 0)
            out.append(v)
        return out

    row, col, slot = ordered(rows), ordered(cols), ordered([jnp.int32(i) for i in range(slots)])
    above = [(row[r] + (SUB - 1)) >> 3 for r in range(slots)]
    below = [jnp.where(r < count, RC - (row[r] >> 3), 0) for r in range(slots)]
    best, cut = jnp.int32(10000), jnp.int32(0)
    for k in range(ITEMS[1] + 1):
        up = sum(above[:k], jnp.int32(0))
        down = sum(below[k:], jnp.int32(0))
        cost = jnp.maximum(up, down)
        bad = (k > count) | (k > most) | (count - k > most)
        cost = jnp.where(bad, 20000, cost)
        cut = jnp.where(cost < best, k, cut)
        best = jnp.minimum(cost, best)

    def listed(first, end, sizes, upward):
        items, off = [], jnp.int32(0)
        for u in range(ITEMS[1]):
            at = first + u
            live = at < end

            def take(vals):
                v = jnp.int32(0)
                for r in range(slots):
                    v = v + jnp.where(live & (at == r), vals[r], 0)
                return v

            n, c = take(sizes), take(col)
            items.append(
                dict(
                    live=jnp.where(live, 1, 0),
                    row=take(row) if upward else jnp.where(live, take(row), PS),
                    block=c >> 7,
                    lane=c & (PS - 1),
                    slot=take(slot),
                    off=off,
                    n=n,
                    base=jnp.int32(0) if upward else RC - n,
                )
            )
            off = off + n
        return items

    return listed(jnp.int32(0), cut, above, True), listed(cut, count, below, False)


def told_slots(ref, slots):
    rows = [ref[0, i] for i in range(slots)]
    return rows, [ref[0, slots + i] for i in range(slots)], ref[0, 2 * slots]


def listings(own, prev, even):
    up_own, down_own = own
    up_prev, down_prev = prev
    sends = [
        [pick(even, a, b) for a, b in zip(down_own, up_prev)],
        [pick(even, a, b) for a, b in zip(up_prev, down_own)],
    ]
    works = [
        [pick(even, a, b) for a, b in zip(up_own, down_prev)],
        [pick(even, a, b) for a, b in zip(down_prev, up_own)],
    ]
    sends = [x[:m] for x, m in zip(sends, ITEMS)]
    works = [x[:m] for x, m in zip(works, ITEMS)]
    return sends, works


def chunk_of(items, j):
    at = [j >= item["off"] for item in items[1:]]

    def choose(vals):
        v = vals[0]
        for later, val in zip(at, vals[1:]):
            v = jnp.where(later, val, v)
        return v

    def get(k):
        return choose([item[k] for item in items])

    r = jnp.clip(j - get("off") + get("base"), 0, RC - 1)
    return get, choose(list(range(len(items)))), r


def split(x):
    hi = x.astype(BF)
    return hi, (x - hi.astype(F32)).astype(BF)


def dot(a, b):
    return jnp.dot(a, b, preferred_element_type=F32)


def grad_kernel(
    count_ref, pos_hbm, tile_hbm, probe_hbm, phase_hbm, diff_hbm, tab_hbm,
    base_ref, near_ref, far_ref, prev_ref, hello_ref,
    pos_ref, tile_ref, probe_ref, kre_ref, kim_ref, diff_ref, tab_ref,
    meta_ref, pack0, pack1, got0, got1, stage_ref, dpack_ref, dgot_ref,
    w0, w1, t0, t1, g_ref, gpack0, gpack1,
    ts, ls, hs, fs, fr, ds, dr, gs_sem, gr_sem,
):
    me, n = lax.axis_index("ty"), lax.axis_size("ty")
    following, previous = lax.rem(me + 1, n), lax.rem(me + n - 1, n)
    even = lax.rem(me, 2) == 0
    peers = [jnp.where(even, following, previous), jnp.where(even, previous, following)]
    pack_ref, got_ref, gpack_ref, theirs_ref = (pack0, pack1), (got0, got1), (gpack0, gpack1), (near_ref, far_ref)
    w_ref, t_ref = (w0, w1), (t0, t1)
    lengths = [pack0.shape[1], pack1.shape[1]]
    blocks = tile_hbm.shape[4] // PS
    last = blocks - 1
    slots = pos_ref.shape[1]

    barrier = pltpu.get_barrier_semaphore()
    for peer in peers:
        pl.semaphore_signal(barrier, inc=1, device_id={"ty": peer}, device_id_type=MESH)

    def tile_copy(s, k):
        return pltpu.make_async_copy(
            tile_hbm.at[s, :, :, :, pl.ds(k * PS, PS)], tile_ref.at[k, s], ts.at[s, k]
        )

    own = pltpu.make_async_copy(pos_hbm, pos_ref, hs.at[3])
    own.start()
    for s in range(NS):
        for k in range(blocks):
            tile_copy(s, k).start()
    loads = [
        pltpu.make_async_copy(probe_hbm, probe_ref, ls.at[0]),
        pltpu.make_async_copy(phase_hbm, kre_ref, ls.at[1]),
        pltpu.make_async_copy(tab_hbm, tab_ref, ls.at[2]),
        pltpu.make_async_copy(diff_hbm, diff_ref, ls.at[3]),
    ]
    for copy in loads:
        copy.start()
    own.wait()
    rows, cols = [pos_ref[0, i] for i in range(slots)], [pos_ref[1, i] for i in range(slots)]
    at = lax.broadcasted_iota(I32, (SUB, PS), 1)
    told = jnp.where(at == 2 * slots, count_ref[0], 0)
    for i in range(slots):
        told = jnp.where(at == i, rows[i], told)
        told = jnp.where(at == slots + i, cols[i], told)
    hello_ref[...] = told
    pl.semaphore_wait(barrier, 2)
    hello = pltpu.make_async_remote_copy(
        src_ref=hello_ref,
        dst_ref=prev_ref,
        send_sem=hs.at[0],
        recv_sem=hs.at[1],
        device_id={"ty": following},
        device_id_type=MESH,
    )
    hello.start()

    row = lax.broadcasted_iota(I32, (PS, PS), 0)
    lane = lax.broadcasted_iota(I32, (PS, PS), 1)
    lane8 = lax.broadcasted_iota(I32, (SUB, PS), 1)

    def fetch(g, s):
        return pltpu.make_async_remote_copy(
            src_ref=pack_ref[g].at[s],
            dst_ref=got_ref[g].at[s],
            send_sem=fs.at[g, s],
            recv_sem=fr.at[g, s],
            device_id={"ty": peers[g]},
            device_id_type=MESH,
        )

    def give(g, s):
        return pltpu.make_async_remote_copy(
            src_ref=gpack_ref[g].at[s],
            dst_ref=theirs_ref[g].at[s],
            send_sem=gs_sem.at[g, s],
            recv_sem=gr_sem.at[g, s],
            device_id={"ty": peers[g]},
            device_id_type=MESH,
        )

    patterns = pltpu.make_async_remote_copy(
        src_ref=dpack_ref,
        dst_ref=dgot_ref,
        send_sem=ds.at[0],
        recv_sem=dr.at[0],
        device_id={"ty": following},
        device_id_type=MESH,
    )

    def send_rows(g, items):
        items = items[: ITEMS[g]]
        table = []
        for j in range(lengths[g]):
            get, _, r = chunk_of(items, j)
            block = get("block")
            table.append((block, jnp.minimum(block + 1, last), get("lane"), r))
        for s in range(NS):
            for j, (here, after, shift, r) in enumerate(table):
                for b in range(2):
                    pack_ref[g][s, j, b] = jnp.where(
                        lane8 >= shift, tile_ref[here, s, b, r], tile_ref[after, s, b, r]
                    )
            fetch(g, s).start()

    up_own, down_own = assign(rows, cols, count_ref[0], even)
    for s in range(NS):
        for k in range(blocks):
            tile_copy(s, k).wait()

    @pl.when(even)
    def _():
        send_rows(0, down_own)

    @pl.when(jnp.logical_not(even))
    def _():
        send_rows(1, down_own)

    hello.wait()
    learn = pltpu.make_async_copy(prev_ref, meta_ref, hs.at[2])
    learn.start()
    for copy in loads:
        copy.wait()
    for u in range(ITEMS[1]):
        dpack_ref[u] = diff_ref[down_own[u]["slot"]]
    learn.wait()
    up_prev, down_prev = assign(*told_slots(meta_ref, slots), jnp.logical_not(even))

    @pl.when(even)
    def _():
        send_rows(1, up_prev)

    @pl.when(jnp.logical_not(even))
    def _():
        send_rows(0, up_prev)

    patterns.start()
    _, works = listings((up_own, down_own), (up_prev, down_prev), even)
    upward = [even, jnp.logical_not(even)]
    phase = kre_ref[...]
    kre_ref[...] = jnp.cos(phase)
    kim_ref[...] = jnp.sin(phase)

    def left(zs, inv):
        hi, lo = tab_ref[2 - 2 * inv], tab_ref[3 - 2 * inv]
        out = []
        for z in zs:
            h, l = split(jnp.concatenate(z, axis=0))
            y = dot(hi, jnp.concatenate([h, l], axis=1))
            y = y[:, :PS] + y[:, PS:] + dot(lo, h)
            out.append((y[:PS], y[PS:]))
        return out

    def right(zs, inv):
        hi, lo = tab_ref[2 * inv], tab_ref[2 * inv + 1]
        out = []
        for z in zs:
            h, l = split(jnp.concatenate(z, axis=1))
            y = dot(h, hi) + dot(l, hi) + dot(h, lo)
            out.append((y[:, :PS], y[:, PS:]))
        return out

    def forward(zs):
        return right(left(zs, 0), 0)

    def backward(zs):
        return left(right(zs, 1), 1)

    def kernel_product(z, sign):
        re, im = z
        kre, kim = kre_ref[...], kim_ref[...] * sign
        return re * kre - im * kim, re * kim + im * kre

    def ours(g, item):
        signed = row * jnp.where(upward[g], 1, -1)
        return signed >= jnp.where(upward[g], item["row"], 1 - item["row"])

    def object_of(g, s):
        stage_ref[pl.ds(RC, lengths[g])] = got_ref[g][s]
        for u, item in enumerate(works[g]):
            here, after = item["block"], jnp.minimum(item["block"] + 1, last)
            start = RC + item["off"] - item["base"]
            mine = ours(g, item)
            for b in range(2):
                own = jnp.where(
                    lane >= item["lane"],
                    tile_ref[here, s, b].reshape(PS, PS),
                    tile_ref[after, s, b].reshape(PS, PS),
                )
                got = jnp.concatenate([stage_ref[start + r, b] for r in range(RC)], axis=0)
                t_ref[g][s, u, b] = jnp.where(mine, own, got)

    def through(g, s):
        zs = []
        for u in range(ITEMS[g]):
            wre, wim, tre, tim = w_ref[g][s, u, 0], w_ref[g][s, u, 1], t_ref[g][s, u, 0], t_ref[g][s, u, 1]
            zs.append((wre * tre - wim * tim, wre * tim + wim * tre))
        return zs

    def ahead(g):
        for u, item in enumerate(works[g]):
            down = item["row"] & (PS - 1)
            for b in range(2):
                w_ref[g][0, u, b] = pltpu.roll(pltpu.roll(probe_ref[b], down, 0), item["lane"], 1)

        def advance(s, carry):
            fetch(g, s).wait_recv()
            object_of(g, s)
            zs = [kernel_product(z, 1.0) for z in forward(through(g, s))]
            for u, z in enumerate(backward(zs)):
                w_ref[g][s + 1, u, 0], w_ref[g][s + 1, u, 1] = z
            return carry

        lax.fori_loop(0, NS - 1, advance, 0)

    def back(g, first):
        items = works[g]
        target = [
            jnp.where(lane8 >= item["lane"], item["block"], item["block"] + 1) for item in items
        ]
        fetch(g, NS - 1).wait_recv()
        object_of(g, NS - 1)
        far = forward(through(g, NS - 1))
        if first:
            patterns.wait_recv()
        grads = []
        for u, (re, im) in enumerate(far):
            item = items[u]
            pattern = jnp.where(upward[g], diff_ref[item["slot"]], dgot_ref[u])
            live = jnp.where(item["live"] > 0, 4.0, 0.0).astype(F32)
            f = (re * re + im * im - pattern) * live
            grads.append((re * f, im * f))
        grads = backward(grads)
        places = []
        for j in range(lengths[g]):
            _, which, r = chunk_of(items, j)
            places.append((which, r))

        def deposit(s, grads):
            mines = []
            for u, (gre, gim) in enumerate(grads):
                mine = ours(g, items[u])
                wre, wim = w_ref[g][s, u, 0], w_ref[g][s, u, 1]
                both = []
                for b, val in enumerate((wre * gre + wim * gim, wre * gim - wim * gre)):
                    both.append(jnp.where(mine, val, 0.0).reshape(RC, SUB, PS))
                    g_ref[u, b] = jnp.where(mine, 0.0, val).reshape(RC, SUB, PS)
                mines.append(both)
            for j, (which, r) in enumerate(places):
                for b in range(2):
                    gpack_ref[g][s, j, b] = g_ref[which, b, r]
            give(g, s).start()
            for k in range(blocks):
                at_k = [(t == k)[None] for t in target]
                for b in range(2):
                    add = sum(jnp.where(m, v[b], 0.0) for m, v in zip(at_k, mines))
                    if first:
                        base_ref[k, s, b] = add
                    else:
                        base_ref[k, s, b] += add

        def retreat(i, grads):
            s = NS - 1 - i
            deposit(s, grads)
            zs = []
            for u, (gre, gim) in enumerate(grads):
                tre, tim = t_ref[g][s, u, 0], t_ref[g][s, u, 1]
                zs.append((gre * tre + gim * tim, gim * tre - gre * tim))
            return tuple(backward([kernel_product(z, -1.0) for z in forward(zs)]))

        grads = lax.fori_loop(0, NS - 1, retreat, tuple(grads))
        deposit(0, grads)

    ahead(0)
    ahead(1)
    back(1, True)
    back(0, False)
    for g in range(2):
        for s in range(NS):
            fetch(g, s).wait_send()
            give(g, s).wait_send()
    patterns.wait_send()
    for g in range(2):
        for s in range(NS):
            give(g, s).wait_recv()


def gradients(count, pos, tile, probe, phase, diff):
    tables = jnp.asarray(dft_parts())
    operands = [
        pltpu.with_memory_space_constraint(x, pltpu.HBM)
        for x in (pos, tile, probe, phase, diff, tables)
    ]
    blocks = tile.shape[4] // PS
    near, far = (NS, SHORT, 2, SUB, PS), (NS, LONG, 2, SUB, PS)
    halves = (blocks, NS, 2, RC, SUB, PS)
    most = max(ITEMS)
    dma = pltpu.SemaphoreType.DMA
    return pl.pallas_call(
        grad_kernel,
        out_shape=(
            jax.ShapeDtypeStruct(halves, F32),
            jax.ShapeDtypeStruct(near, F32),
            jax.ShapeDtypeStruct(far, F32),
            jax.ShapeDtypeStruct((SUB, PS), I32),
            jax.ShapeDtypeStruct((SUB, PS), I32),
        ),
        in_specs=[SMEM] + [pl.BlockSpec(memory_space=pltpu.HBM)] * len(operands),
        out_specs=(VMEM,) * 5,
        scratch_shapes=[
            pltpu.SMEM(pos.shape, I32),
            pltpu.VMEM(halves, F32),
            pltpu.VMEM((2, PS, PS), F32),
            pltpu.VMEM((PS, PS), F32),
            pltpu.VMEM((PS, PS), F32),
            pltpu.VMEM(diff.shape, F32),
            pltpu.VMEM(tables.shape, BF),
            pltpu.SMEM((SUB, PS), I32),
            pltpu.VMEM(near, F32),
            pltpu.VMEM(far, F32),
            pltpu.VMEM(near, F32),
            pltpu.VMEM(far, F32),
            pltpu.VMEM((max(SHORT, LONG) + 2 * RC, 2, SUB, PS), F32),
            pltpu.VMEM((most, PS, PS), F32),
            pltpu.VMEM((most, PS, PS), F32),
            pltpu.VMEM((NS, ITEMS[0], 2, PS, PS), F32),
            pltpu.VMEM((NS, ITEMS[1], 2, PS, PS), F32),
            pltpu.VMEM((NS, ITEMS[0], 2, PS, PS), F32),
            pltpu.VMEM((NS, ITEMS[1], 2, PS, PS), F32),
            pltpu.VMEM((most, 2, RC, SUB, PS), F32),
            pltpu.VMEM(near, F32),
            pltpu.VMEM(far, F32),
            dma((NS, blocks)),
            dma((4,)),
            dma((4,)),
            dma((2, NS)),
            dma((2, NS)),
            dma((1,)),
            dma((1,)),
            dma((2, NS)),
            dma((2, NS)),
        ],
        compiler_params=pltpu.CompilerParams(
            collective_id=0, has_side_effects=True, vmem_limit_bytes=40 << 20
        ),
        cost_estimate=pl.CostEstimate(flops=8 * 10**9, bytes_accessed=5 * 10**6, transcendentals=0),
    )(count, *operands)


def place_kernel(slots, own_ref, prev_ref, base_ref, near_ref, far_ref, out_hbm, sum_ref, own_s, prev_s, sems):
    even = lax.rem(lax.axis_index("ty"), 2) == 0
    theirs_ref = (near_ref, far_ref)
    learn = [
        pltpu.make_async_copy(own_ref, own_s, sems.at[NS]),
        pltpu.make_async_copy(prev_ref, prev_s, sems.at[NS + 1]),
    ]
    for copy in learn:
        copy.start()
    for copy in learn:
        copy.wait()
    own = assign(*told_slots(own_s, slots), even)
    prev = assign(*told_slots(prev_s, slots), jnp.logical_not(even))
    sends, _ = listings(own, prev, even)
    blocks = base_ref.shape[0]
    lane8 = lax.broadcasted_iota(I32, (SUB, PS), 1)
    copies = []
    for s in range(NS):
        for k in range(blocks):
            for b in range(2):
                sum_ref[s, b, :, :, k * PS : (k + 1) * PS] = base_ref[k, s, b]
        for g in range(2):
            for item in sends[g]:
                block = item["block"]
                here = pl.ds(pl.multiple_of(block * PS, PS), PS)
                after = pl.ds(pl.multiple_of(jnp.minimum(block + 1, blocks - 1) * PS, PS), PS)

                def add(i, carry):
                    r, j = item["base"] + i, item["off"] + i
                    got = [theirs_ref[g][s, j, b] for b in range(2)]
                    old = [(sum_ref[s, b, r, :, here]) for b in range(2)]
                    for b in range(2):
                        sum_ref[s, b, r, :, here] = old[b] + jnp.where(lane8 >= item["lane"], got[b], 0.0)
                    old = [(sum_ref[s, b, r, :, after]) for b in range(2)]
                    for b in range(2):
                        sum_ref[s, b, r, :, after] = old[b] + jnp.where(lane8 >= item["lane"], 0.0, got[b])
                    return carry

                lax.fori_loop(0, item["n"], add, 0)
        copy = pltpu.make_async_copy(sum_ref.at[s], out_hbm.at[s], sems.at[s])
        copy.start()
        copies.append(copy)
    for copy in copies:
        copy.wait()


def place(slots, own, prev, base, near, far):
    shape = (NS, 2, RC, SUB, base.shape[0] * PS)
    return pl.pallas_call(
        functools.partial(place_kernel, slots),
        in_specs=[VMEM] * 5,
        out_specs=pl.BlockSpec(memory_space=pltpu.HBM),
        out_shape=jax.ShapeDtypeStruct(shape, F32),
        scratch_shapes=[
            pltpu.VMEM(shape, F32),
            pltpu.SMEM((SUB, PS), I32),
            pltpu.SMEM((SUB, PS), I32),
            pltpu.SemaphoreType.DMA((NS + 2,)),
        ],
        compiler_params=pltpu.CompilerParams(vmem_limit_bytes=16 << 20),
        cost_estimate=pl.CostEstimate(flops=10**6, bytes_accessed=7 * 10**6, transcendentals=0),
    )(own, prev, base, near, far)


def per_device(tile_object, probe_wave, propagator_phase, diffraction, positions, counts):
    width = tile_object.shape[3]
    pos = positions.T
    tile = tile_object.reshape(NS, 2, RC, SUB, width)
    base, near, far, prev, own = gradients(counts, pos, tile, probe_wave, propagator_phase, diffraction)
    return place(positions.shape[0], own, prev, base, near, far).reshape(tile_object.shape)


def solution(mesh):
    in_specs = (
        P(None, None, ("grp", "ty"), None),
        P(),
        P(),
        P(("grp", "ty"), None, None),
        P(("grp", "ty"), None),
        P(("grp", "ty")),
    )
    out_specs = P(None, None, ("grp", "ty"), None)
    return jax.shard_map(
        per_device, mesh=mesh, in_specs=in_specs, out_specs=out_specs, check_vma=False
    )
```

```python
import functools

import jax
import jax.numpy as jnp
import numpy as np
from jax import lax
from jax.experimental import pallas as pl
from jax.experimental.pallas import tpu as pltpu
from jax.sharding import PartitionSpec as P

PS = 128
NS = 4
SUB = 8
RC = PS // SUB
ITEMS = (2, 3)
SHORT = 2 * RC
LEVELS = (14, 16, 20)
SQUAD = 4
BF = jnp.bfloat16
F32 = jnp.float32
I32 = jnp.int32
VMEM = pl.BlockSpec(memory_space=pltpu.VMEM)
SMEM = pl.BlockSpec(memory_space=pltpu.SMEM)
MESH = pl.DeviceIdType.MESH


def dft_parts():
    k = np.arange(PS)
    ang = (np.outer(k, k) % PS) * (2.0 * np.pi / PS)
    c = np.cos(ang) / np.sqrt(PS)
    s = -np.sin(ang) / np.sqrt(PS)
    forward = np.block([[c, s], [-s, c]]).astype(np.float32)
    inverse = np.block([[c, -s], [s, c]]).astype(np.float32)
    parts = []
    for m in (forward, inverse):
        hi = m.astype(BF)
        lo = (m - hi.astype(np.float32)).astype(BF)
        parts += [hi, lo]
    return np.stack(parts)


def pick(flag, a, b):
    return {k: jnp.where(flag, a[k], b[k]) for k in a}


def assign(rows, cols, count, even):
    most = jnp.where(even, ITEMS[0], ITEMS[1])
    slots = len(rows)
    key = [jnp.where(i < count, rows[i], 1000) for i in range(slots)]
    rank = []
    for i in range(slots):
        r = jnp.int32(0)
        for j in range(slots):
            if j != i:
                ahead = key[j] <= key[i] if j < i else key[j] < key[i]
                r = r + jnp.where(ahead, 1, 0)
        rank.append(r)

    def ordered(vals):
        out = []
        for r in range(slots):
            v = jnp.int32(0)
            for i in range(slots):
                v = v + jnp.where(rank[i] == r, vals[i], 0)
            out.append(v)
        return out

    row, col, slot = ordered(rows), ordered(cols), ordered([jnp.int32(i) for i in range(slots)])
    above = [(row[r] + (SUB - 1)) >> 3 for r in range(slots)]
    below = [jnp.where(r < count, RC - (row[r] >> 3), 0) for r in range(slots)]
    best, cut = jnp.int32(10000), jnp.int32(0)
    for k in range(ITEMS[1] + 1):
        up = sum(above[:k], jnp.int32(0))
        down = sum(below[k:], jnp.int32(0))
        cost = jnp.maximum(up, down)
        bad = (k > count) | (k > most) | (count - k > most)
        cost = jnp.where(bad, 20000, cost)
        cut = jnp.where(cost < best, k, cut)
        best = jnp.minimum(cost, best)

    def listed(first, end, sizes, upward):
        items, off = [], jnp.int32(0)
        for u in range(ITEMS[1]):
            at = first + u
            live = at < end

            def take(vals):
                v = jnp.int32(0)
                for r in range(slots):
                    v = v + jnp.where(live & (at == r), vals[r], 0)
                return v

            n, c = take(sizes), take(col)
            items.append(
                dict(
                    live=jnp.where(live, 1, 0),
                    row=take(row) if upward else jnp.where(live, take(row), PS),
                    block=c >> 7,
                    lane=c & (PS - 1),
                    slot=take(slot),
                    off=off,
                    n=n,
                    base=jnp.int32(0) if upward else RC - n,
                )
            )
            off = off + n
        return items

    return listed(jnp.int32(0), cut, above, True), listed(cut, count, below, False), best


def told_slots(ref, slots):
    rows = [ref[0, i] for i in range(slots)]
    return rows, [ref[0, slots + i] for i in range(slots)], ref[0, 2 * slots]


def listings(own, prev, even):
    up_own, down_own, _ = own
    up_prev, down_prev, _ = prev
    sends = [
        [pick(even, a, b) for a, b in zip(down_own, up_prev)],
        [pick(even, a, b) for a, b in zip(up_prev, down_own)],
    ]
    works = [
        [pick(even, a, b) for a, b in zip(up_own, down_prev)],
        [pick(even, a, b) for a, b in zip(down_prev, up_own)],
    ]
    sends = [x[:m] for x, m in zip(sends, ITEMS)]
    works = [x[:m] for x, m in zip(works, ITEMS)]
    return sends, works


def chunk_of(items, j):
    at = [j >= item["off"] for item in items[1:]]

    def choose(vals):
        v = vals[0]
        for later, val in zip(at, vals[1:]):
            v = jnp.where(later, val, v)
        return v

    def get(k):
        return choose([item[k] for item in items])

    r = jnp.clip(j - get("off") + get("base"), 0, RC - 1)
    return get, choose(list(range(len(items)))), r


def split(x):
    hi = x.astype(BF)
    return hi, (x - hi.astype(F32)).astype(BF)


def dot(a, b):
    return jnp.dot(a, b, preferred_element_type=F32)


def transforms(tab_ref, kre_ref, kim_ref):
    def left(zs, inv):
        hi, lo = tab_ref[2 - 2 * inv], tab_ref[3 - 2 * inv]
        out = []
        for z in zs:
            h, l = split(jnp.concatenate(z, axis=0))
            y = dot(hi, jnp.concatenate([h, l], axis=1))
            y = y[:, :PS] + y[:, PS:] + dot(lo, h)
            out.append((y[:PS], y[PS:]))
        return out

    def right(zs, inv):
        hi, lo = tab_ref[2 * inv], tab_ref[2 * inv + 1]
        out = []
        for z in zs:
            h, l = split(jnp.concatenate(z, axis=1))
            y = dot(h, hi) + dot(l, hi) + dot(h, lo)
            out.append((y[:, :PS], y[:, PS:]))
        return out

    def forward(zs):
        return right(left(zs, 0), 0)

    def backward(zs):
        return left(right(zs, 1), 1)

    def kernel_product(z, sign):
        re, im = z
        kre, kim = kre_ref[...], kim_ref[...] * sign
        return re * kre - im * kim, re * kim + im * kre

    return forward, backward, kernel_product


def neighbours():
    me, n = lax.axis_index("ty"), lax.axis_size("ty")
    following, previous = lax.rem(me + 1, n), lax.rem(me + n - 1, n)
    even = lax.rem(me, 2) == 0
    peers = [jnp.where(even, following, previous), jnp.where(even, previous, following)]
    return peers, even, following, previous


def remote(src, dst, sends, receives, to):
    return pltpu.make_async_remote_copy(
        src_ref=src, dst_ref=dst, send_sem=sends, recv_sem=receives, device_id=to, device_id_type=MESH
    )


class Group:
    def __init__(self, g, works, even, tile_ref, w_ref, t_ref, stage_ref, g_ref, maths):
        self.items, self.tile, self.w, self.t = works[g], tile_ref, w_ref, t_ref
        self.stage, self.g, self.maths = stage_ref, g_ref, maths
        self.up = even if g == 0 else jnp.logical_not(even)
        self.row = lax.broadcasted_iota(I32, (PS, PS), 0)
        self.lane = lax.broadcasted_iota(I32, (PS, PS), 1)
        self.lane8 = lax.broadcasted_iota(I32, (SUB, PS), 1)
        self.last = tile_ref.shape[0] - 1

    def ours(self, item):
        signed = self.row * jnp.where(self.up, 1, -1)
        return signed >= jnp.where(self.up, item["row"], 1 - item["row"])

    def object_of(self, s, got):
        at = RC
        for part in got:
            self.stage[pl.ds(at, part.shape[1])] = part[s]
            at += part.shape[1]
        for u, item in enumerate(self.items):
            here, after = item["block"], jnp.minimum(item["block"] + 1, self.last)
            start = RC + item["off"] - item["base"]
            mine = self.ours(item)
            for b in range(2):
                own = jnp.where(
                    self.lane >= item["lane"],
                    self.tile[here, s, b].reshape(PS, PS),
                    self.tile[after, s, b].reshape(PS, PS),
                )
                rest = jnp.concatenate([self.stage[start + r, b] for r in range(RC)], axis=0)
                self.t[s, u, b] = jnp.where(mine, own, rest)

    def through(self, s):
        zs = []
        for u in range(len(self.items)):
            wre, wim, tre, tim = self.w[s, u, 0], self.w[s, u, 1], self.t[s, u, 0], self.t[s, u, 1]
            zs.append((wre * tre - wim * tim, wre * tim + wim * tre))
        return zs

    def start(self, probe_ref):
        for u, item in enumerate(self.items):
            down = item["row"] & (PS - 1)
            for b in range(2):
                self.w[0, u, b] = pltpu.roll(pltpu.roll(probe_ref[b], down, 0), item["lane"], 1)

    def ahead(self, arrive, got):
        forward, backward, kernel_product = self.maths

        def advance(s, carry):
            arrive(s)
            self.object_of(s, got)
            zs = [kernel_product(z, 1.0) for z in forward(self.through(s))]
            for u, z in enumerate(backward(zs)):
                self.w[s + 1, u, 0], self.w[s + 1, u, 1] = z
            return carry

        lax.fori_loop(0, NS - 1, advance, 0)
        arrive(NS - 1)
        self.object_of(NS - 1, got)

    def back(self, length, pattern_of, pack, give, keep, write=None):
        forward, backward, kernel_product = self.maths
        items = self.items
        target = [
            jnp.where(self.lane8 >= item["lane"], item["block"], item["block"] + 1) for item in items
        ]
        grads = []
        for u, (re, im) in enumerate(forward(self.through(NS - 1))):
            pattern = pattern_of(u)
            live = jnp.where(items[u]["live"] > 0, 4.0, 0.0).astype(F32)
            f = (re * re + im * im - pattern) * live
            grads.append((re * f, im * f))
        grads = backward(grads)
        places = []
        for j in range(length):
            _, which, r = chunk_of(items, j)
            places.append((which, r))

        def deposit(s, grads):
            mines = []
            for u, (gre, gim) in enumerate(grads):
                mine = self.ours(items[u])
                wre, wim = self.w[s, u, 0], self.w[s, u, 1]
                both = []
                for b, val in enumerate((wre * gre + wim * gim, wre * gim - wim * gre)):
                    both.append(jnp.where(mine, val, 0.0).reshape(RC, SUB, PS))
                    self.g[u, b] = jnp.where(mine, 0.0, val).reshape(RC, SUB, PS)
                mines.append(both)
            for j, (which, r) in enumerate(places):
                for b in range(2):
                    pack(s, j, b, self.g[which, b, r])
            give(s).start()
            for k in range(self.last + 1):
                at_k = [(t == k)[None] for t in target]
                for b in range(2):
                    add = sum(jnp.where(m, v[b], 0.0) for m, v in zip(at_k, mines))
                    keep(k, s, b, add)
            if write is not None:
                write(s).start()

        def retreat(i, grads):
            s = NS - 1 - i
            deposit(s, grads)
            zs = []
            for u, (gre, gim) in enumerate(grads):
                tre, tim = self.t[s, u, 0], self.t[s, u, 1]
                zs.append((gre * tre + gim * tim, gim * tre - gre * tim))
            return tuple(backward([kernel_product(z, -1.0) for z in forward(zs)]))

        grads = lax.fori_loop(0, NS - 1, retreat, tuple(grads))
        deposit(0, grads)


def pack_rows(pack_ref, tile_ref, items, first, send):
    last = tile_ref.shape[0] - 1
    lane8 = lax.broadcasted_iota(I32, (SUB, PS), 1)
    table = []
    for j in range(pack_ref.shape[1]):
        get, _, r = chunk_of(items, first + j)
        block = get("block")
        table.append((block, jnp.minimum(block + 1, last), get("lane"), r))
    for s in range(NS):
        for j, (here, after, shift, r) in enumerate(table):
            for b in range(2):
                pack_ref[s, j, b] = jnp.where(
                    lane8 >= shift, tile_ref[here, s, b, r], tile_ref[after, s, b, r]
                )
        send(s).start()


def first_kernel(
    count_ref, pos_hbm, tile_hbm, probe_hbm, phase_hbm, diff_hbm, tab_hbm,
    level_ref, base_ref, near_ref, prev_ref, hello_ref, tile_ref, w1, t1, got1, dgot_ref,
    diff_ref, tab_ref, kre_ref, kim_ref,
    pos_ref, probe_ref, meta_ref, pack0, pack1, got0, stage_ref, dpack_ref,
    w0, t0, g_ref, p_ref, gpack0, squad, all_ref,
    ts, ls, hs, fs, fr, ds, gs_sem, gr_sem, sq,
):
    peers, even, following, previous = neighbours()
    tiles, parts = lax.axis_size("ty"), lax.axis_size("grp")
    me = lax.axis_index("grp") * tiles + lax.axis_index("ty")
    squads = tiles * parts // SQUAD
    place, rank = me // SQUAD, lax.rem(me, SQUAD)
    blocks = tile_hbm.shape[4] // PS
    slots = pos_ref.shape[1]
    pack_ref, got_ref = (pack0, pack1), (got0, got1)

    def device(to):
        return {"grp": to // tiles, "ty": lax.rem(to, tiles)}

    mates = [device(place * SQUAD + lax.rem(rank + k, SQUAD)) for k in range(1, SQUAD)]
    fellows = [device(lax.rem(place + k, squads) * SQUAD + rank) for k in range(1, squads)]

    barrier = pltpu.get_barrier_semaphore()
    for to in [{"ty": peer} for peer in peers] + mates + fellows:
        pl.semaphore_signal(barrier, inc=1, device_id=to, device_id_type=MESH)

    def tile_copy(s, k):
        return pltpu.make_async_copy(
            tile_hbm.at[s, :, :, :, pl.ds(k * PS, PS)], tile_ref.at[k, s], ts.at[s, k]
        )

    own = pltpu.make_async_copy(pos_hbm, pos_ref, hs.at[3])
    own.start()
    for s in range(NS):
        for k in range(blocks):
            tile_copy(s, k).start()
    loads = [
        pltpu.make_async_copy(probe_hbm, probe_ref, ls.at[0]),
        pltpu.make_async_copy(phase_hbm, kre_ref, ls.at[1]),
        pltpu.make_async_copy(tab_hbm, tab_ref, ls.at[2]),
        pltpu.make_async_copy(diff_hbm, diff_ref, ls.at[3]),
    ]
    for copy in loads:
        copy.start()
    own.wait()
    rows, cols = [pos_ref[0, i] for i in range(slots)], [pos_ref[1, i] for i in range(slots)]
    at = lax.broadcasted_iota(I32, (SUB, PS), 1)
    told = jnp.where(at == 2 * slots, count_ref[0], 0)
    for i in range(slots):
        told = jnp.where(at == i, rows[i], told)
        told = jnp.where(at == slots + i, cols[i], told)
    hello_ref[...] = told
    pl.semaphore_wait(barrier, 2 + len(mates) + len(fellows))
    hello = remote(hello_ref, prev_ref, hs.at[0], hs.at[1], {"ty": following})
    hello.start()

    def fetch(g, s):
        return remote(pack_ref[g].at[s], got_ref[g].at[s], fs.at[g, s], fr.at[g, s], {"ty": peers[g]})

    def give(s):
        return remote(gpack0.at[s], near_ref.at[s], gs_sem.at[s], gr_sem.at[s], {"ty": peers[0]})

    patterns = remote(dpack_ref, dgot_ref, ds.at[0], ds.at[1], {"ty": following})

    mine = assign(rows, cols, count_ref[0], even)
    down_own = mine[1]
    squad[rank] = jnp.zeros((1, PS), I32) + jnp.where(even, 0, mine[2])
    shouts = [remote(squad.at[rank], squad.at[rank], sq.at[0], sq.at[1], to) for to in mates]
    for copy in shouts:
        copy.start()
    for s in range(NS):
        for k in range(blocks):
            tile_copy(s, k).wait()

    def send_rows(g, items):
        pack_rows(pack_ref[g], tile_ref, items[: ITEMS[g]], 0, functools.partial(fetch, g))

    @pl.when(even)
    def _():
        send_rows(0, down_own)

    @pl.when(jnp.logical_not(even))
    def _():
        send_rows(1, down_own)

    hello.wait()
    learn = pltpu.make_async_copy(prev_ref, meta_ref, hs.at[2])
    learn.start()
    for copy in loads:
        copy.wait()
    for u in range(ITEMS[1]):
        dpack_ref[u] = diff_ref[down_own[u]["slot"]]
    learn.wait()
    prev = assign(*told_slots(meta_ref, slots), jnp.logical_not(even))

    @pl.when(even)
    def _():
        send_rows(1, prev[0])

    @pl.when(jnp.logical_not(even))
    def _():
        send_rows(0, prev[0])

    patterns.start()
    _, works = listings(mine, prev, even)
    phase = kre_ref[...]
    kre_ref[...] = jnp.cos(phase)
    kim_ref[...] = jnp.sin(phase)
    maths = transforms(tab_ref, kre_ref, kim_ref)
    chip = Group(0, works, even, tile_ref, w0, t0, stage_ref, g_ref, maths)
    edge = Group(1, works, even, tile_ref, w1, t1, stage_ref, g_ref, maths)
    chip.start(probe_ref)
    edge.start(probe_ref)

    def settle(ref, count, sem):
        part = ref.at[pl.ds(0, count)]
        pltpu.make_async_copy(part, part, sem).wait()

    settle(squad, SQUAD - 1, sq.at[1])
    settle(squad, SQUAD - 1, sq.at[0])
    all_ref[place] = jnp.max(squad[...], axis=0)
    for to in fellows:
        remote(all_ref.at[place], all_ref.at[place], sq.at[2], sq.at[3], to).start()

    chip.ahead(lambda s: fetch(0, s).wait_recv(), [got0])

    @pl.when(even)
    def _():
        for u, item in enumerate(works[0]):
            p_ref[u] = diff_ref[item["slot"]]

    @pl.when(jnp.logical_not(even))
    def _():
        patterns.wait_recv()
        for u in range(ITEMS[0]):
            p_ref[u] = dgot_ref[u]

    def pack(s, j, b, val):
        gpack0[s, j, b] = val

    def keep(k, s, b, val):
        base_ref[k, s, b] = val

    chip.back(pack0.shape[1], lambda u: p_ref[u], pack, give, keep)
    settle(all_ref, squads - 1, sq.at[3])
    settle(all_ref, squads - 1, sq.at[2])
    most = jnp.max(jnp.max(all_ref[...], axis=0))
    level = jnp.int32(0)
    for bound in LEVELS[:-1]:
        level = level + jnp.where(most > bound, 1, 0)
    level_ref[0] = level
    edge.ahead(lambda s: fetch(1, s).wait_recv(), [got1])

    @pl.when(even)
    def _():
        patterns.wait_recv()

    for s in range(NS):
        give(s).wait_send()
        give(s).wait_recv()
        for g in range(2):
            fetch(g, s).wait_send()
    patterns.wait_send()


def first_part(count, pos, tile, probe, phase, diff):
    tables = jnp.asarray(dft_parts())
    operands = [
        pltpu.with_memory_space_constraint(x, pltpu.HBM)
        for x in (pos, tile, probe, phase, diff, tables)
    ]
    blocks = tile.shape[4] // PS
    near, far = (NS, SHORT, 2, SUB, PS), (NS, LEVELS[0], 2, SUB, PS)
    halves = (blocks, NS, 2, RC, SUB, PS)
    few, most = ITEMS
    every = lax.axis_size("ty") * lax.axis_size("grp")
    dma = pltpu.SemaphoreType.DMA
    return pl.pallas_call(
        first_kernel,
        out_shape=(
            jax.ShapeDtypeStruct((1,), I32),
            jax.ShapeDtypeStruct(halves, F32),
            jax.ShapeDtypeStruct(near, F32),
            jax.ShapeDtypeStruct((SUB, PS), I32),
            jax.ShapeDtypeStruct((SUB, PS), I32),
            jax.ShapeDtypeStruct(halves, F32),
            jax.ShapeDtypeStruct((NS, most, 2, PS, PS), F32),
            jax.ShapeDtypeStruct((NS, most, 2, PS, PS), F32),
            jax.ShapeDtypeStruct(far, F32),
            jax.ShapeDtypeStruct((most, PS, PS), F32),
            jax.ShapeDtypeStruct(diff.shape, F32),
            jax.ShapeDtypeStruct(tables.shape, BF),
            jax.ShapeDtypeStruct((PS, PS), F32),
            jax.ShapeDtypeStruct((PS, PS), F32),
        ),
        in_specs=[SMEM] + [pl.BlockSpec(memory_space=pltpu.HBM)] * len(operands),
        out_specs=(SMEM,) + (VMEM,) * 13,
        scratch_shapes=[
            pltpu.SMEM(pos.shape, I32),
            pltpu.VMEM((2, PS, PS), F32),
            pltpu.SMEM((SUB, PS), I32),
            pltpu.VMEM(near, F32),
            pltpu.VMEM(far, F32),
            pltpu.VMEM(near, F32),
            pltpu.VMEM((SHORT + 2 * RC, 2, SUB, PS), F32),
            pltpu.VMEM((most, PS, PS), F32),
            pltpu.VMEM((NS, few, 2, PS, PS), F32),
            pltpu.VMEM((NS, few, 2, PS, PS), F32),
            pltpu.VMEM((few, 2, RC, SUB, PS), F32),
            pltpu.VMEM((few, PS, PS), F32),
            pltpu.VMEM(near, F32),
            pltpu.VMEM((SQUAD, 1, PS), I32),
            pltpu.VMEM((every // SQUAD, 1, PS), I32),
            dma((NS, blocks)),
            dma((4,)),
            dma((4,)),
            dma((2, NS)),
            dma((2, NS)),
            dma((2,)),
            dma((NS,)),
            dma((NS,)),
            dma((4,)),
        ],
        compiler_params=pltpu.CompilerParams(
            collective_id=0, has_side_effects=True, vmem_limit_bytes=20 << 20
        ),
        cost_estimate=pl.CostEstimate(flops=5 * 10**9, bytes_accessed=5 * 10**6, transcendentals=0),
    )(count, *operands)


def second_kernel(
    slots, length, prev_ref, hello_ref, before_ref, tile_ref, wa, ta, got_ref, dgot_ref, diff_ref,
    tab_ref, kre_ref, kim_ref,
    sum_hbm, far_hbm,
    own_s, prev_s, stage_ref, g_ref, gpack_ref, sum_ref, sem, gs_sem, gr_sem, out_sem, *more,
):
    peers, even, _, _ = neighbours()
    barrier = pltpu.get_barrier_semaphore()
    for peer in peers:
        pl.semaphore_signal(barrier, inc=1, device_id={"ty": peer}, device_id_type=MESH)
    learn = [
        pltpu.make_async_copy(hello_ref, own_s, sem.at[0]),
        pltpu.make_async_copy(prev_ref, prev_s, sem.at[1]),
    ]
    for copy in learn:
        copy.start()
    for copy in learn:
        copy.wait()
    own = assign(*told_slots(own_s, slots), even)
    prev = assign(*told_slots(prev_s, slots), jnp.logical_not(even))
    sends, works = listings(own, prev, even)
    pl.semaphore_wait(barrier, 2)

    def give(s):
        landing = far_hbm.at[s, pl.ds(0, 2 * length)]
        return remote(gpack_ref.at[s], landing, gs_sem.at[s], gr_sem.at[s], {"ty": peers[1]})

    def pack(s, j, b, val):
        gpack_ref[s, 2 * j + b] = val

    def keep(k, s, b, val):
        sum_ref[s, b, :, :, k * PS : (k + 1) * PS] = before_ref[k, s, b] + val

    def write(s):
        return pltpu.make_async_copy(sum_ref.at[s], sum_hbm.at[s], out_sem.at[s])

    maths = transforms(tab_ref, kre_ref, kim_ref)
    had = got_ref.shape[1]
    if length > had:
        wb, tb, pack_ref, rest_ref, fs, fr = more

        def fetch(s):
            return remote(pack_ref.at[s], rest_ref.at[s], fs.at[s], fr.at[s], {"ty": peers[1]})

        pack_rows(pack_ref, tile_ref, sends[1], had, fetch)
        edge = Group(1, works, even, tile_ref, wb, tb, stage_ref, g_ref, maths)
        wb[0] = wa[0]
        edge.ahead(lambda s: fetch(s).wait_recv(), [got_ref, rest_ref])
        for s in range(NS):
            fetch(s).wait_send()
    else:
        edge = Group(1, works, even, tile_ref, wa, ta, stage_ref, g_ref, maths)

    def pattern_of(u):
        return jnp.where(edge.up, diff_ref[works[1][u]["slot"]], dgot_ref[u])

    edge.back(length, pattern_of, pack, give, keep, write)
    for s in range(NS):
        write(s).wait()
        give(s).wait_send()
        give(s).wait_recv()


def second_part(level, slots, *operands):
    tile, got = operands[3], operands[6]
    length, had = LEVELS[level], got.shape[1]
    full = (NS, 2, RC, SUB, tile.shape[0] * PS)
    most = ITEMS[1]
    dma = pltpu.SemaphoreType.DMA
    scratch = [
        pltpu.SMEM((SUB, PS), I32),
        pltpu.SMEM((SUB, PS), I32),
        pltpu.VMEM((length + 2 * RC, 2, SUB, PS), F32),
        pltpu.VMEM((most, 2, RC, SUB, PS), F32),
        pltpu.VMEM((NS, 2 * length, SUB, PS), F32),
        pltpu.VMEM(full, F32),
        dma((2,)),
        dma((NS,)),
        dma((NS,)),
        dma((NS,)),
    ]
    if length > had:
        scratch += [
            pltpu.VMEM((NS, most, 2, PS, PS), F32),
            pltpu.VMEM((NS, most, 2, PS, PS), F32),
            pltpu.VMEM((NS, length - had, 2, SUB, PS), F32),
            pltpu.VMEM((NS, length - had, 2, SUB, PS), F32),
            dma((NS,)),
            dma((NS,)),
        ]
    return pl.pallas_call(
        functools.partial(second_kernel, slots, length),
        out_shape=(
            jax.ShapeDtypeStruct(full, F32),
            jax.ShapeDtypeStruct((NS, 2 * LEVELS[-1], SUB, PS), F32),
        ),
        in_specs=[VMEM] * len(operands),
        out_specs=(pl.BlockSpec(memory_space=pltpu.HBM),) * 2,
        scratch_shapes=scratch,
        compiler_params=pltpu.CompilerParams(
            collective_id=1 + level, has_side_effects=True, vmem_limit_bytes=20 << 20
        ),
        cost_estimate=pl.CostEstimate(flops=3 * 10**9, bytes_accessed=5 * 10**6, transcendentals=0),
    )(*operands)


def place_kernel(slots, own_ref, prev_ref, near_ref, sum_hbm, far_hbm, out_hbm, sum_ref, far_ref, own_s, prev_s, sems):
    even = lax.rem(lax.axis_index("ty"), 2) == 0
    blocks = sum_ref.shape[4] // PS
    learn = [
        pltpu.make_async_copy(own_ref, own_s, sems.at[0]),
        pltpu.make_async_copy(prev_ref, prev_s, sems.at[1]),
    ]
    arrive = pltpu.make_async_copy(far_hbm, far_ref, sems.at[2])
    reads = [pltpu.make_async_copy(sum_hbm.at[s], sum_ref.at[s], sems.at[3 + s]) for s in range(NS)]
    for copy in learn + [arrive] + reads:
        copy.start()
    for copy in learn:
        copy.wait()

    def theirs(g, s, j, b):
        return near_ref[s, j, b] if g == 0 else far_ref[s, 2 * j + b]

    own = assign(*told_slots(own_s, slots), even)
    prev = assign(*told_slots(prev_s, slots), jnp.logical_not(even))
    sends, _ = listings(own, prev, even)
    arrive.wait()
    lane8 = lax.broadcasted_iota(I32, (SUB, PS), 1)
    copies = []
    for s in range(NS):
        reads[s].wait()
        for g in range(2):
            for item in sends[g]:
                block = item["block"]
                here = pl.ds(pl.multiple_of(block * PS, PS), PS)
                after = pl.ds(pl.multiple_of(jnp.minimum(block + 1, blocks - 1) * PS, PS), PS)

                def add(i, carry):
                    r, j = item["base"] + i, item["off"] + i
                    got = [theirs(g, s, j, b) for b in range(2)]
                    old = [(sum_ref[s, b, r, :, here]) for b in range(2)]
                    for b in range(2):
                        sum_ref[s, b, r, :, here] = old[b] + jnp.where(lane8 >= item["lane"], got[b], 0.0)
                    old = [(sum_ref[s, b, r, :, after]) for b in range(2)]
                    for b in range(2):
                        sum_ref[s, b, r, :, after] = old[b] + jnp.where(lane8 >= item["lane"], 0.0, got[b])
                    return carry

                lax.fori_loop(0, item["n"], add, 0)
        copy = pltpu.make_async_copy(sum_ref.at[s], out_hbm.at[s], sems.at[3 + NS + s])
        copy.start()
        copies.append(copy)
    for copy in copies:
        copy.wait()


def place(slots, own, prev, near, total, far):
    hbm = pl.BlockSpec(memory_space=pltpu.HBM)
    return pl.pallas_call(
        functools.partial(place_kernel, slots),
        in_specs=[VMEM] * 3 + [hbm] * 2,
        out_specs=pl.BlockSpec(memory_space=pltpu.HBM),
        out_shape=jax.ShapeDtypeStruct(total.shape, F32),
        scratch_shapes=[
            pltpu.VMEM(total.shape, F32),
            pltpu.VMEM(far.shape, F32),
            pltpu.SMEM((SUB, PS), I32),
            pltpu.SMEM((SUB, PS), I32),
            pltpu.SemaphoreType.DMA((3 + 2 * NS,)),
        ],
        compiler_params=pltpu.CompilerParams(vmem_limit_bytes=16 << 20),
        cost_estimate=pl.CostEstimate(flops=10**6, bytes_accessed=7 * 10**6, transcendentals=0),
    )(own, prev, near, *[pltpu.with_memory_space_constraint(x, pltpu.HBM) for x in (total, far)])


def per_device(tile_object, probe_wave, propagator_phase, diffraction, positions, counts):
    width = tile_object.shape[3]
    pos = positions.T
    tile = tile_object.reshape(NS, 2, RC, SUB, width)
    slots = positions.shape[0]
    level, base, near, prev, own, *rest = first_part(
        counts, pos, tile, probe_wave, propagator_phase, diffraction
    )

    def branch(i):
        return lambda *args: second_part(i, slots, *args)

    total, far = lax.switch(level[0], [branch(i) for i in range(len(LEVELS))], prev, own, base, *rest)
    return place(slots, own, prev, near, total, far).reshape(tile_object.shape)


def solution(mesh):
    in_specs = (
        P(None, None, ("grp", "ty"), None),
        P(),
        P(),
        P(("grp", "ty"), None, None),
        P(("grp", "ty"), None),
        P(("grp", "ty")),
    )
    out_specs = P(None, None, ("grp", "ty"), None)
    return jax.shard_map(
        per_device, mesh=mesh, in_specs=in_specs, out_specs=out_specs, check_vma=False
    )
```

```python
import functools

import jax
import jax.numpy as jnp
import numpy as np
from jax import lax
from jax.experimental import pallas as pl
from jax.experimental.pallas import tpu as pltpu
from jax.sharding import PartitionSpec as P

PS = 128
NS = 4
SUB = 8
RC = PS // SUB
ITEMS = (2, 3)
SHORT = 2 * RC
LEVELS = (14, 16, 20)
SQUAD = 4
BF = jnp.bfloat16
F32 = jnp.float32
I32 = jnp.int32
VMEM = pl.BlockSpec(memory_space=pltpu.VMEM)
SMEM = pl.BlockSpec(memory_space=pltpu.SMEM)
MESH = pl.DeviceIdType.MESH


def dft_parts():
    k = np.arange(PS)
    ang = (np.outer(k, k) % PS) * (2.0 * np.pi / PS)
    c = np.cos(ang) / np.sqrt(PS)
    s = -np.sin(ang) / np.sqrt(PS)
    forward = np.block([[c, s], [-s, c]]).astype(np.float32)
    inverse = np.block([[c, -s], [s, c]]).astype(np.float32)
    parts = []
    for m in (forward, inverse):
        hi = m.astype(BF)
        lo = (m - hi.astype(np.float32)).astype(BF)
        parts += [hi, lo]
    return np.stack(parts)


def pick(flag, a, b):
    return {k: jnp.where(flag, a[k], b[k]) for k in a}


def assign(rows, cols, count, even):
    most = jnp.where(even, ITEMS[0], ITEMS[1])
    slots = len(rows)
    key = [jnp.where(i < count, rows[i], 1000) for i in range(slots)]
    rank = []
    for i in range(slots):
        r = jnp.int32(0)
        for j in range(slots):
            if j != i:
                ahead = key[j] <= key[i] if j < i else key[j] < key[i]
                r = r + jnp.where(ahead, 1, 0)
        rank.append(r)

    def ordered(vals):
        out = []
        for r in range(slots):
            v = jnp.int32(0)
            for i in range(slots):
                v = v + jnp.where(rank[i] == r, vals[i], 0)
            out.append(v)
        return out

    row, col, slot = ordered(rows), ordered(cols), ordered([jnp.int32(i) for i in range(slots)])
    above = [(row[r] + (SUB - 1)) >> 3 for r in range(slots)]
    below = [jnp.where(r < count, RC - (row[r] >> 3), 0) for r in range(slots)]
    best, cut = jnp.int32(10000), jnp.int32(0)
    for k in range(ITEMS[1] + 1):
        up = sum(above[:k], jnp.int32(0))
        down = sum(below[k:], jnp.int32(0))
        cost = jnp.maximum(up, down)
        cost = jnp.where(count - k > ITEMS[0], jnp.maximum(cost, LEVELS[0] + 1), cost)
        bad = (k > count) | (k > most) | (count - k > most)
        cost = jnp.where(bad, 20000, cost)
        cut = jnp.where(cost < best, k, cut)
        best = jnp.minimum(cost, best)

    def listed(first, end, sizes, upward):
        items, off = [], jnp.int32(0)
        for u in range(ITEMS[1]):
            at = first + u
            live = at < end

            def take(vals):
                v = jnp.int32(0)
                for r in range(slots):
                    v = v + jnp.where(live & (at == r), vals[r], 0)
                return v

            n, c = take(sizes), take(col)
            items.append(
                dict(
                    live=jnp.where(live, 1, 0),
                    row=take(row) if upward else jnp.where(live, take(row), PS),
                    block=c >> 7,
                    lane=c & (PS - 1),
                    slot=take(slot),
                    off=off,
                    n=n,
                    base=jnp.int32(0) if upward else RC - n,
                )
            )
            off = off + n
        return items

    return listed(jnp.int32(0), cut, above, True), listed(cut, count, below, False), best


def told_slots(ref, slots):
    rows = [ref[0, i] for i in range(slots)]
    return rows, [ref[0, slots + i] for i in range(slots)], ref[0, 2 * slots]


def listings(own, prev, even):
    up_own, down_own, _ = own
    up_prev, down_prev, _ = prev
    sends = [
        [pick(even, a, b) for a, b in zip(down_own, up_prev)],
        [pick(even, a, b) for a, b in zip(up_prev, down_own)],
    ]
    works = [
        [pick(even, a, b) for a, b in zip(up_own, down_prev)],
        [pick(even, a, b) for a, b in zip(down_prev, up_own)],
    ]
    sends = [x[:m] for x, m in zip(sends, ITEMS)]
    works = [x[:m] for x, m in zip(works, ITEMS)]
    return sends, works


FIELDS = ("live", "row", "block", "lane", "slot", "off", "n", "base")


def to_row(works, sends, third):
    items = works[0] + works[1] + sends[0] + sends[1]
    at = lax.broadcasted_iota(I32, (SUB, PS), 1)
    row = jnp.zeros((SUB, PS), I32)
    for i, val in enumerate([item[f] for item in items for f in FIELDS] + [third]):
        row = jnp.where(at == i, val, row)
    return row


def from_row(ref):
    count = 2 * sum(ITEMS)
    items = [{f: ref[0, i * len(FIELDS) + k] for k, f in enumerate(FIELDS)} for i in range(count)]
    cuts = [0, ITEMS[0], sum(ITEMS), sum(ITEMS) + ITEMS[0], count]
    a, b, c, d = [items[i:j] for i, j in zip(cuts[:-1], cuts[1:])]
    return (a, b), (c, d), ref[0, count * len(FIELDS)]


def chunk_of(items, j):
    at = [j >= item["off"] for item in items[1:]]

    def choose(vals):
        v = vals[0]
        for later, val in zip(at, vals[1:]):
            v = jnp.where(later, val, v)
        return v

    def get(k):
        return choose([item[k] for item in items])

    r = jnp.clip(j - get("off") + get("base"), 0, RC - 1)
    return get, choose(list(range(len(items)))), r


def split(x):
    hi = x.astype(BF)
    return hi, (x - hi.astype(F32)).astype(BF)


def dot(a, b):
    return jnp.dot(a, b, preferred_element_type=F32)


def transforms(tab_ref, kre_ref, kim_ref):
    def left(zs, inv):
        hi, lo = tab_ref[2 - 2 * inv], tab_ref[3 - 2 * inv]
        out = []
        for z in zs:
            h, l = split(jnp.concatenate(z, axis=0))
            y = dot(hi, jnp.concatenate([h, l], axis=1))
            y = y[:, :PS] + y[:, PS:] + dot(lo, h)
            out.append((y[:PS], y[PS:]))
        return out

    def right(zs, inv):
        hi, lo = tab_ref[2 * inv], tab_ref[2 * inv + 1]
        out = []
        for z in zs:
            h, l = split(jnp.concatenate(z, axis=1))
            y = dot(h, hi) + dot(l, hi) + dot(h, lo)
            out.append((y[:, :PS], y[:, PS:]))
        return out

    def forward(zs):
        return right(left(zs, 0), 0)

    def backward(zs):
        return left(right(zs, 1), 1)

    def kernel_product(z, sign):
        re, im = z
        kre, kim = kre_ref[...], kim_ref[...] * sign
        return re * kre - im * kim, re * kim + im * kre

    return forward, backward, kernel_product


def neighbours():
    me, n = lax.axis_index("ty"), lax.axis_size("ty")
    following, previous = lax.rem(me + 1, n), lax.rem(me + n - 1, n)
    even = lax.rem(me, 2) == 0
    peers = [jnp.where(even, following, previous), jnp.where(even, previous, following)]
    return peers, even, following, previous


def remote(src, dst, sends, receives, to):
    return pltpu.make_async_remote_copy(
        src_ref=src, dst_ref=dst, send_sem=sends, recv_sem=receives, device_id=to, device_id_type=MESH
    )


class Group:
    def __init__(self, g, works, even, tile_ref, w_ref, t_ref, stage_ref, g_ref, maths):
        self.items, self.tile, self.w, self.t = works[g], tile_ref, w_ref, t_ref
        self.stage, self.g, self.maths = stage_ref, g_ref, maths
        self.up = even if g == 0 else jnp.logical_not(even)
        self.row = lax.broadcasted_iota(I32, (PS, PS), 0)
        self.lane = lax.broadcasted_iota(I32, (PS, PS), 1)
        self.lane8 = lax.broadcasted_iota(I32, (SUB, PS), 1)
        self.last = tile_ref[0].shape[0] - 1

    def ours(self, item):
        signed = self.row * jnp.where(self.up, 1, -1)
        return signed >= jnp.where(self.up, item["row"], 1 - item["row"])

    def object_of(self, s, got):
        at = RC
        for part in got:
            self.stage[pl.ds(at, part.shape[1])] = part[s]
            at += part.shape[1]
        for u, item in enumerate(self.items):
            here, after = item["block"], jnp.minimum(item["block"] + 1, self.last)
            start = RC + item["off"] - item["base"]
            mine = self.ours(item)
            for b in range(2):
                own = jnp.where(
                    self.lane >= item["lane"],
                    self.tile[s][here, b].reshape(PS, PS),
                    self.tile[s][after, b].reshape(PS, PS),
                )
                rest = jnp.concatenate([self.stage[start + r, b] for r in range(RC)], axis=0)
                self.t[s, u, b] = jnp.where(mine, own, rest)

    def through(self, s):
        zs = []
        for u in range(len(self.items)):
            wre, wim, tre, tim = self.w[s, u, 0], self.w[s, u, 1], self.t[s, u, 0], self.t[s, u, 1]
            zs.append((wre * tre - wim * tim, wre * tim + wim * tre))
        return zs

    def start(self, probe_ref):
        for u, item in enumerate(self.items):
            down = item["row"] & (PS - 1)
            for b in range(2):
                self.w[0, u, b] = pltpu.roll(pltpu.roll(probe_ref[b], down, 0), item["lane"], 1)

    def ahead(self, arrive, got):
        forward, backward, kernel_product = self.maths

        for s in range(NS - 1):
            arrive(s)
            self.object_of(s, got)
            zs = [kernel_product(z, 1.0) for z in forward(self.through(s))]
            for u, z in enumerate(backward(zs)):
                self.w[s + 1, u, 0], self.w[s + 1, u, 1] = z
        arrive(NS - 1)
        self.object_of(NS - 1, got)

    def back(self, length, pattern_of, pack, give, keep, write=None):
        forward, backward, kernel_product = self.maths
        items = self.items
        target = [
            jnp.where(self.lane8 >= item["lane"], item["block"], item["block"] + 1) for item in items
        ]
        grads = []
        for u, (re, im) in enumerate(forward(self.through(NS - 1))):
            pattern = pattern_of(u)
            live = jnp.where(items[u]["live"] > 0, 4.0, 0.0).astype(F32)
            f = (re * re + im * im - pattern) * live
            grads.append((re * f, im * f))
        grads = backward(grads)
        places = []
        for j in range(length):
            _, which, r = chunk_of(items, j)
            places.append((which, r))

        def deposit(s, grads):
            mines = []
            for u, (gre, gim) in enumerate(grads):
                mine = self.ours(items[u])
                wre, wim = self.w[s, u, 0], self.w[s, u, 1]
                both = []
                for b, val in enumerate((wre * gre + wim * gim, wre * gim - wim * gre)):
                    both.append(jnp.where(mine, val, 0.0).reshape(RC, SUB, PS))
                    self.g[u, b] = jnp.where(mine, 0.0, val).reshape(RC, SUB, PS)
                mines.append(both)
            for j, (which, r) in enumerate(places):
                for b in range(2):
                    pack(s, j, b, self.g[which, b, r])
            give(s).start()
            for k in range(self.last + 1):
                at_k = [(t == k)[None] for t in target]
                for b in range(2):
                    add = sum(jnp.where(m, v[b], 0.0) for m, v in zip(at_k, mines))
                    keep(k, s, b, add)
            if write is not None:
                write(s).start()

        def retreat(i, grads):
            s = NS - 1 - i
            deposit(s, grads)
            zs = []
            for u, (gre, gim) in enumerate(grads):
                tre, tim = self.t[s, u, 0], self.t[s, u, 1]
                zs.append((gre * tre + gim * tim, gim * tre - gre * tim))
            return tuple(backward([kernel_product(z, -1.0) for z in forward(zs)]))

        grads = lax.fori_loop(0, NS - 1, retreat, tuple(grads))
        deposit(0, grads)


def pack_rows(pack_ref, tile_ref, items, first, send, ready=lambda s: None):
    last = tile_ref[0].shape[0] - 1
    lane8 = lax.broadcasted_iota(I32, (SUB, PS), 1)
    table = []
    for j in range(pack_ref.shape[1]):
        get, _, r = chunk_of(items, first + j)
        block = get("block")
        table.append((block, jnp.minimum(block + 1, last), get("lane"), r))
    for s in range(NS):
        ready(s)
        for j, (here, after, shift, r) in enumerate(table):
            for b in range(2):
                pack_ref[s, j, b] = jnp.where(
                    lane8 >= shift, tile_ref[s][here, b, r], tile_ref[s][after, b, r]
                )
        send(s).start()


def first_kernel(
    count_ref, pos_hbm, tile_hbm, probe_hbm, phase_hbm, diff_hbm, tab_hbm,
    level_ref, table_ref, tile0, tile1, tile2, tile3, w0, t0, w1, t1, got1, dgot_ref,
    diff_ref, tab_ref, kre_ref, kim_ref,
    pos_ref, probe_ref, prev_ref, hello_ref, meta_ref, pack0, pack1, got0, stage_ref, dpack_ref,
    squad, all_ref,
    ts, ls, hs, fs, fr, ds, sq,
):
    peers, even, following, previous = neighbours()
    tiles, parts = lax.axis_size("ty"), lax.axis_size("grp")
    me = lax.axis_index("grp") * tiles + lax.axis_index("ty")
    squads = tiles * parts // SQUAD
    place, rank = me // SQUAD, lax.rem(me, SQUAD)
    blocks = tile_hbm.shape[4] // PS
    slots = pos_ref.shape[1]
    pack_ref, got_ref = (pack0, pack1), (got0, got1)

    def device(to):
        return {"grp": to // tiles, "ty": lax.rem(to, tiles)}

    mates = [device(place * SQUAD + lax.rem(rank + k, SQUAD)) for k in range(1, SQUAD)]
    fellows = [device(lax.rem(place + k, squads) * SQUAD + rank) for k in range(1, squads)]

    owns = [
        pltpu.make_async_copy(pos_hbm, pos_ref, hs.at[3]),
    ]
    for copy in owns:
        copy.start()
    barrier = pltpu.get_barrier_semaphore()
    for to in [{"ty": peer} for peer in peers] + mates + fellows:
        pl.semaphore_signal(barrier, inc=1, device_id=to, device_id_type=MESH)

    tile_ref = (tile0, tile1, tile2, tile3)

    def tile_copy(s, k):
        return pltpu.make_async_copy(
            tile_hbm.at[s, :, :, :, pl.ds(k * PS, PS)], tile_ref[s].at[k], ts.at[s, k]
        )

    for s in range(NS):
        for k in range(blocks):
            tile_copy(s, k).start()
    loads = [
        pltpu.make_async_copy(probe_hbm, probe_ref, ls.at[0]),
        pltpu.make_async_copy(phase_hbm, kre_ref, ls.at[1]),
        pltpu.make_async_copy(tab_hbm, tab_ref, ls.at[2]),
        pltpu.make_async_copy(diff_hbm, diff_ref, ls.at[3]),
    ]
    for copy in loads:
        copy.start()
    for copy in owns:
        copy.wait()
    count = count_ref[0]
    rows, cols = [pos_ref[0, i] for i in range(slots)], [pos_ref[1, i] for i in range(slots)]
    at = lax.broadcasted_iota(I32, (SUB, PS), 1)
    told = jnp.where(at == 2 * slots, count, 0)
    for i in range(slots):
        told = jnp.where(at == i, rows[i], told)
        told = jnp.where(at == slots + i, cols[i], told)
    hello_ref[...] = told
    pl.semaphore_wait(barrier, 2 + len(mates) + len(fellows))
    hello = remote(hello_ref, prev_ref, hs.at[0], hs.at[1], {"ty": following})
    hello.start()

    def fetch(g, s):
        return remote(pack_ref[g].at[s], got_ref[g].at[s], fs.at[g, s], fr.at[g, s], {"ty": peers[g]})

    patterns = remote(dpack_ref, dgot_ref, ds.at[0], ds.at[1], {"ty": following})

    mine = assign(rows, cols, count, even)
    down_own = mine[1]
    squad[rank] = jnp.zeros((1, PS), I32) + jnp.where(even, 0, mine[2])
    shouts = [remote(squad.at[rank], squad.at[rank], sq.at[0], sq.at[1], to) for to in mates]
    for copy in shouts:
        copy.start()

    def send_rows(g, items, ready=lambda s: None):
        pack_rows(pack_ref[g], tile_ref, items[: ITEMS[g]], 0, functools.partial(fetch, g), ready)

    def loaded(s):
        for k in range(blocks):
            tile_copy(s, k).wait()

    @pl.when(even)
    def _():
        send_rows(0, down_own, loaded)

    @pl.when(jnp.logical_not(even))
    def _():
        send_rows(1, down_own, loaded)

    hello.wait()
    learn = pltpu.make_async_copy(prev_ref, meta_ref, hs.at[2])
    learn.start()
    for copy in loads:
        copy.wait()
    for u in range(ITEMS[0]):
        dpack_ref[u] = diff_ref[down_own[u]["slot"]]
    learn.wait()
    prev = assign(*told_slots(meta_ref, slots), jnp.logical_not(even))

    @pl.when(even)
    def _():
        send_rows(1, prev[0])

    @pl.when(jnp.logical_not(even))
    def _():
        send_rows(0, prev[0])

    patterns.start()
    sends, works = listings(mine, prev, even)
    table_ref[...] = to_row(works, sends, down_own[ITEMS[0]]["slot"])
    phase = kre_ref[...]
    kre_ref[...] = jnp.cos(phase)
    kim_ref[...] = jnp.sin(phase)
    maths = transforms(tab_ref, kre_ref, kim_ref)
    chip = Group(0, works, even, tile_ref, w0, t0, stage_ref, None, maths)
    edge = Group(1, works, even, tile_ref, w1, t1, stage_ref, None, maths)
    chip.start(probe_ref)
    edge.start(probe_ref)

    def settle(ref, count, sem):
        part = ref.at[pl.ds(0, count)]
        pltpu.make_async_copy(part, part, sem).wait()

    settle(squad, SQUAD - 1, sq.at[1])
    settle(squad, SQUAD - 1, sq.at[0])
    all_ref[place] = jnp.max(squad[...], axis=0)
    for to in fellows:
        remote(all_ref.at[place], all_ref.at[place], sq.at[2], sq.at[3], to).start()

    chip.ahead(lambda s: fetch(0, s).wait_recv(), [got0])

    settle(all_ref, squads - 1, sq.at[3])
    settle(all_ref, squads - 1, sq.at[2])
    most = jnp.max(jnp.max(all_ref[...], axis=0))
    level = jnp.int32(0)
    for bound in LEVELS[:-1]:
        level = level + jnp.where(most > bound, 1, 0)
    level_ref[0] = level
    edge.ahead(lambda s: fetch(1, s).wait_recv(), [got1])
    for s in range(NS):
        for g in range(2):
            fetch(g, s).wait_send()
    patterns.wait()


def first_part(count, pos, tile, probe, phase, diff):
    tables = jnp.asarray(dft_parts())
    operands = [
        pltpu.with_memory_space_constraint(x, pltpu.HBM)
        for x in (pos, tile, probe, phase, diff, tables)
    ]
    blocks = tile.shape[4] // PS
    near, far = (NS, SHORT, 2, SUB, PS), (NS, LEVELS[0], 2, SUB, PS)
    few, most = ITEMS
    every = lax.axis_size("ty") * lax.axis_size("grp")
    dma = pltpu.SemaphoreType.DMA
    return pl.pallas_call(
        first_kernel,
        out_shape=(
            jax.ShapeDtypeStruct((1,), I32),
            jax.ShapeDtypeStruct((SUB, PS), I32),
        )
        + (jax.ShapeDtypeStruct((blocks, 2, RC, SUB, PS), F32),) * NS
        + (
            jax.ShapeDtypeStruct((NS, few, 2, PS, PS), F32),
            jax.ShapeDtypeStruct((NS, few, 2, PS, PS), F32),
            jax.ShapeDtypeStruct((NS, most, 2, PS, PS), F32),
            jax.ShapeDtypeStruct((NS, most, 2, PS, PS), F32),
            jax.ShapeDtypeStruct(far, F32),
            jax.ShapeDtypeStruct((few, PS, PS), F32),
            jax.ShapeDtypeStruct(diff.shape, F32),
            jax.ShapeDtypeStruct(tables.shape, BF),
            jax.ShapeDtypeStruct((PS, PS), F32),
            jax.ShapeDtypeStruct((PS, PS), F32),
        ),
        in_specs=[SMEM] + [pl.BlockSpec(memory_space=pltpu.HBM)] * len(operands),
        out_specs=(SMEM,) + (VMEM,) * (11 + NS),
        scratch_shapes=[
            pltpu.SMEM(pos.shape, I32),
            pltpu.VMEM((2, PS, PS), F32),
            pltpu.VMEM((SUB, PS), I32),
            pltpu.VMEM((SUB, PS), I32),
            pltpu.SMEM((SUB, PS), I32),
            pltpu.VMEM(near, F32),
            pltpu.VMEM(far, F32),
            pltpu.VMEM(near, F32),
            pltpu.VMEM((SHORT + 2 * RC, 2, SUB, PS), F32),
            pltpu.VMEM((few, PS, PS), F32),
            pltpu.VMEM((SQUAD, 1, PS), I32),
            pltpu.VMEM((every // SQUAD, 1, PS), I32),
            dma((NS, blocks)),
            dma((4,)),
            dma((5,)),
            dma((2, NS)),
            dma((2, NS)),
            dma((2,)),
            dma((4,)),
        ],
        compiler_params=pltpu.CompilerParams(
            collective_id=0, has_side_effects=True, vmem_limit_bytes=20 << 20
        ),
        cost_estimate=pl.CostEstimate(flops=5 * 10**9, bytes_accessed=5 * 10**6, transcendentals=0),
    )(count, *operands)


def second_kernel(
    length, table_ref, tile0, tile1, tile2, tile3, w0, t0, wa, ta, got_ref, dgot_ref, diff_ref,
    tab_ref, kre_ref, kim_ref,
    sum_hbm, near_hbm, far_hbm,
    table_s, stage_ref, g_ref, gpack0, gpack1, sum_ref, sem, gs_sem, gr_sem, out_sem, *more,
):
    peers, even, following, _ = neighbours()
    tile_ref = (tile0, tile1, tile2, tile3)
    barrier = pltpu.get_barrier_semaphore()
    for peer in peers:
        pl.semaphore_signal(barrier, inc=1, device_id={"ty": peer}, device_id_type=MESH)
    learn = pltpu.make_async_copy(table_ref, table_s, sem.at[0])
    learn.start()
    learn.wait()
    works, sends, third = from_row(table_s)
    pl.semaphore_wait(barrier, 2)

    gpacks, landings = (gpack0, gpack1), (near_hbm, far_hbm)

    def give(g, s):
        landing = landings[g].at[s, pl.ds(0, gpacks[g].shape[1])]
        return remote(gpacks[g].at[s], landing, gs_sem.at[g, s], gr_sem.at[g, s], {"ty": peers[g]})

    def pack(g, s, j, b, val):
        gpacks[g][s, 2 * j + b] = val

    def keep(g, k, s, b, val):
        if g == 1:
            sum_ref[s, b, :, :, k * PS : (k + 1) * PS] = val
        else:
            sum_ref[s, b, :, :, k * PS : (k + 1) * PS] += val

    def write(s):
        return pltpu.make_async_copy(sum_ref.at[s], sum_hbm.at[s], out_sem.at[s])

    maths = transforms(tab_ref, kre_ref, kim_ref)
    had = got_ref.shape[1]
    if length > had:
        wb, tb, pack_ref, rest_ref, dpack_ref, drest_ref, fs, fr, ds = more
        patterns = remote(dpack_ref, drest_ref, ds.at[0], ds.at[1], {"ty": following})
        dpack_ref[...] = diff_ref[third]

        def fetch(s):
            return remote(pack_ref.at[s], rest_ref.at[s], fs.at[s], fr.at[s], {"ty": peers[1]})

        pack_rows(pack_ref, tile_ref, sends[1], had, fetch)
        patterns.start()
        edge = Group(1, works, even, tile_ref, wb, tb, stage_ref, g_ref, maths)
        wb[0] = wa[0]
        edge.ahead(lambda s: fetch(s).wait_recv(), [got_ref, rest_ref])
        patterns.wait()
        for s in range(NS):
            fetch(s).wait_send()
    else:
        edge = Group(1, works, even, tile_ref, wa, ta, stage_ref, g_ref, maths)

    def pattern_of(group, u):
        mine = diff_ref[group.items[u]["slot"]]
        if u < ITEMS[0]:
            return jnp.where(group.up, mine, dgot_ref[u])
        return jnp.where(group.up, mine, drest_ref[...]) if length > had else mine

    chip = Group(0, works, even, tile_ref, w0, t0, stage_ref, g_ref, maths)
    for g, group, size, done in ((1, edge, length, None), (0, chip, SHORT, write)):
        group.back(
            size,
            functools.partial(pattern_of, group),
            functools.partial(pack, g),
            functools.partial(give, g),
            functools.partial(keep, g),
            done,
        )
    for s in range(NS):
        write(s).wait()
        for g in range(2):
            give(g, s).wait_send()
            give(g, s).wait_recv()


def second_part(level, *operands):
    tile, got = operands[1], operands[5 + NS]
    length, had = LEVELS[level], got.shape[1]
    full = (NS, 2, RC, SUB, tile.shape[0] * PS)
    most = ITEMS[1]
    dma = pltpu.SemaphoreType.DMA
    scratch = [
        pltpu.SMEM((SUB, PS), I32),
        pltpu.VMEM((length + 2 * RC, 2, SUB, PS), F32),
        pltpu.VMEM((most, 2, RC, SUB, PS), F32),
        pltpu.VMEM((NS, 2 * SHORT, SUB, PS), F32),
        pltpu.VMEM((NS, 2 * length, SUB, PS), F32),
        pltpu.VMEM(full, F32),
        dma((1,)),
        dma((2, NS)),
        dma((2, NS)),
        dma((NS,)),
    ]
    if length > had:
        scratch += [
            pltpu.VMEM((NS, most, 2, PS, PS), F32),
            pltpu.VMEM((NS, most, 2, PS, PS), F32),
            pltpu.VMEM((NS, length - had, 2, SUB, PS), F32),
            pltpu.VMEM((NS, length - had, 2, SUB, PS), F32),
            pltpu.VMEM((PS, PS), F32),
            pltpu.VMEM((PS, PS), F32),
            dma((NS,)),
            dma((NS,)),
            dma((2,)),
        ]
    return pl.pallas_call(
        functools.partial(second_kernel, length),
        out_shape=(
            jax.ShapeDtypeStruct(full, F32),
            jax.ShapeDtypeStruct((NS, 2 * SHORT, SUB, PS), F32),
            jax.ShapeDtypeStruct((NS, 2 * LEVELS[-1], SUB, PS), F32),
        ),
        in_specs=[VMEM] * len(operands),
        out_specs=(pl.BlockSpec(memory_space=pltpu.HBM),) * 3,
        scratch_shapes=scratch,
        compiler_params=pltpu.CompilerParams(
            collective_id=1 + level, has_side_effects=True, vmem_limit_bytes=20 << 20
        ),
        cost_estimate=pl.CostEstimate(flops=3 * 10**9, bytes_accessed=5 * 10**6, transcendentals=0),
    )(*operands)


def place_kernel(table_ref, sum_hbm, near_hbm, far_hbm, out_hbm, sum_ref, near_ref, far_ref, table_s, sems):
    blocks = sum_ref.shape[4] // PS
    learn = pltpu.make_async_copy(table_ref, table_s, sems.at[0])
    arrive = [
        pltpu.make_async_copy(near_hbm, near_ref, sems.at[1]),
        pltpu.make_async_copy(far_hbm, far_ref, sems.at[2]),
    ]
    reads = [pltpu.make_async_copy(sum_hbm.at[s], sum_ref.at[s], sems.at[3 + s]) for s in range(NS)]
    for copy in [learn] + arrive + reads:
        copy.start()
    learn.wait()

    def theirs(g, s, j, b):
        return (near_ref, far_ref)[g][s, 2 * j + b]

    _, sends, _ = from_row(table_s)
    for copy in arrive:
        copy.wait()
    lane8 = lax.broadcasted_iota(I32, (SUB, PS), 1)
    copies = []
    for pair in (range(s, s + 2) for s in range(0, NS, 2)):
        for s in pair:
            reads[s].wait()
        for g in range(2):
            for item in sends[g]:
                block, shift = item["block"], item["lane"]
                here = pl.ds(pl.multiple_of(block * PS, PS), PS)
                after = pl.ds(pl.multiple_of(jnp.minimum(block + 1, blocks - 1) * PS, PS), PS)

                def add(i, carry):
                    r, j = item["base"] + i, item["off"] + i
                    planes = [(s, b) for s in pair for b in range(2)]
                    got = [theirs(g, s, j, b) for s, b in planes]
                    old = [sum_ref[s, b, r, :, here] for s, b in planes]
                    for (s, b), x, y in zip(planes, old, got):
                        sum_ref[s, b, r, :, here] = x + jnp.where(lane8 >= shift, y, 0.0)
                    old = [sum_ref[s, b, r, :, after] for s, b in planes]
                    for (s, b), x, y in zip(planes, old, got):
                        sum_ref[s, b, r, :, after] = x + jnp.where(lane8 >= shift, 0.0, y)
                    return carry

                lax.fori_loop(0, item["n"], add, 0)
        for s in pair:
            copy = pltpu.make_async_copy(sum_ref.at[s], out_hbm.at[s], sems.at[3 + NS + s])
            copy.start()
            copies.append(copy)
    for copy in copies:
        copy.wait()


def place(table, total, near, far):
    hbm = pl.BlockSpec(memory_space=pltpu.HBM)
    return pl.pallas_call(
        place_kernel,
        in_specs=[VMEM] + [hbm] * 3,
        out_specs=pl.BlockSpec(memory_space=pltpu.HBM),
        out_shape=jax.ShapeDtypeStruct(total.shape, F32),
        scratch_shapes=[
            pltpu.VMEM(total.shape, F32),
            pltpu.VMEM(near.shape, F32),
            pltpu.VMEM(far.shape, F32),
            pltpu.SMEM((SUB, PS), I32),
            pltpu.SemaphoreType.DMA((3 + 2 * NS,)),
        ],
        compiler_params=pltpu.CompilerParams(vmem_limit_bytes=16 << 20),
        cost_estimate=pl.CostEstimate(flops=10**6, bytes_accessed=7 * 10**6, transcendentals=0),
    )(table, *[pltpu.with_memory_space_constraint(x, pltpu.HBM) for x in (total, near, far)])


def per_device(tile_object, probe_wave, propagator_phase, diffraction, positions, counts):
    width = tile_object.shape[3]
    pos = positions.T
    tile = tile_object.reshape(NS, 2, RC, SUB, width)
    level, table, *rest = first_part(
        counts, pos, tile, probe_wave, propagator_phase, diffraction
    )

    def branch(i):
        return lambda *args: second_part(i, *args)

    total, near, far = lax.switch(level[0], [branch(i) for i in range(len(LEVELS))], table, *rest)
    return place(table, total, near, far).reshape(tile_object.shape)


def solution(mesh):
    in_specs = (
        P(None, None, ("grp", "ty"), None),
        P(),
        P(),
        P(("grp", "ty"), None, None),
        P(("grp", "ty"), None),
        P(("grp", "ty")),
    )
    out_specs = P(None, None, ("grp", "ty"), None)
    return jax.shard_map(
        per_device, mesh=mesh, in_specs=in_specs, out_specs=out_specs, check_vma=False
    )
```

```python
import functools

import jax
import jax.numpy as jnp
import numpy as np
from jax import lax
from jax.experimental import pallas as pl
from jax.experimental.pallas import tpu as pltpu
from jax.sharding import PartitionSpec as P

PS = 128
NS = 4
SUB = 8
RC = PS // SUB
ITEMS = (2, 3)
SHORT = 2 * RC
LEVELS = (14, 16, 20)
SQUAD = 4
BF = jnp.bfloat16
F32 = jnp.float32
I32 = jnp.int32
VMEM = pl.BlockSpec(memory_space=pltpu.VMEM)
SMEM = pl.BlockSpec(memory_space=pltpu.SMEM)
MESH = pl.DeviceIdType.MESH


def dft_parts():
    k = np.arange(PS)
    ang = (np.outer(k, k) % PS) * (2.0 * np.pi / PS)
    c = np.cos(ang) / np.sqrt(PS)
    s = -np.sin(ang) / np.sqrt(PS)
    forward = np.block([[c, s], [-s, c]]).astype(np.float32)
    inverse = np.block([[c, -s], [s, c]]).astype(np.float32)
    parts = []
    for m in (forward, inverse):
        hi = m.astype(BF)
        lo = (m - hi.astype(np.float32)).astype(BF)
        parts += [hi, lo]
    return np.stack(parts)


def pick(flag, a, b):
    return {k: jnp.where(flag, a[k], b[k]) for k in a}


def assign(rows, cols, count, even):
    most = jnp.where(even, ITEMS[0], ITEMS[1])
    slots = len(rows)
    key = [jnp.where(i < count, rows[i], 1000) for i in range(slots)]
    rank = []
    for i in range(slots):
        r = jnp.int32(0)
        for j in range(slots):
            if j != i:
                ahead = key[j] <= key[i] if j < i else key[j] < key[i]
                r = r + jnp.where(ahead, 1, 0)
        rank.append(r)

    def ordered(vals):
        out = []
        for r in range(slots):
            v = jnp.int32(0)
            for i in range(slots):
                v = v + jnp.where(rank[i] == r, vals[i], 0)
            out.append(v)
        return out

    row, col, slot = ordered(rows), ordered(cols), ordered([jnp.int32(i) for i in range(slots)])
    above = [(row[r] + (SUB - 1)) >> 3 for r in range(slots)]
    below = [jnp.where(r < count, RC - (row[r] >> 3), 0) for r in range(slots)]
    best, cut = jnp.int32(10000), jnp.int32(0)
    for k in range(ITEMS[1] + 1):
        up = sum(above[:k], jnp.int32(0))
        down = sum(below[k:], jnp.int32(0))
        cost = jnp.maximum(up, down)
        bad = (k > count) | (k > most) | (count - k > most)
        cost = jnp.where(bad, 20000, cost)
        cut = jnp.where(cost < best, k, cut)
        best = jnp.minimum(cost, best)

    def listed(first, end, sizes, upward):
        items, off = [], jnp.int32(0)
        for u in range(ITEMS[1]):
            at = first + u
            live = at < end

            def take(vals):
                v = jnp.int32(0)
                for r in range(slots):
                    v = v + jnp.where(live & (at == r), vals[r], 0)
                return v

            n, c = take(sizes), take(col)
            items.append(
                dict(
                    live=jnp.where(live, 1, 0),
                    row=take(row) if upward else jnp.where(live, take(row), PS),
                    block=c >> 7,
                    lane=c & (PS - 1),
                    slot=take(slot),
                    off=off,
                    n=n,
                    base=jnp.int32(0) if upward else RC - n,
                )
            )
            off = off + n
        return items

    return listed(jnp.int32(0), cut, above, True), listed(cut, count, below, False), best


def told_slots(ref, slots):
    rows = [ref[0, i] for i in range(slots)]
    return rows, [ref[0, slots + i] for i in range(slots)], ref[0, 2 * slots]


def listings(own, prev, even):
    up_own, down_own, _ = own
    up_prev, down_prev, _ = prev
    sends = [
        [pick(even, a, b) for a, b in zip(down_own, up_prev)],
        [pick(even, a, b) for a, b in zip(up_prev, down_own)],
    ]
    works = [
        [pick(even, a, b) for a, b in zip(up_own, down_prev)],
        [pick(even, a, b) for a, b in zip(down_prev, up_own)],
    ]
    sends = [x[:m] for x, m in zip(sends, ITEMS)]
    works = [x[:m] for x, m in zip(works, ITEMS)]
    return sends, works


FIELDS = ("live", "row", "block", "lane", "slot", "off", "n", "base")


def to_row(works, sends):
    items = works[0] + works[1] + sends[0] + sends[1]
    at = lax.broadcasted_iota(I32, (SUB, PS), 1)
    row = jnp.zeros((SUB, PS), I32)
    for i, val in enumerate([item[f] for item in items for f in FIELDS]):
        row = jnp.where(at == i, val, row)
    return row


def from_row(ref):
    count = 2 * sum(ITEMS)
    items = [{f: ref[0, i * len(FIELDS) + k] for k, f in enumerate(FIELDS)} for i in range(count)]
    cuts = [0, ITEMS[0], sum(ITEMS), sum(ITEMS) + ITEMS[0], count]
    a, b, c, d = [items[i:j] for i, j in zip(cuts[:-1], cuts[1:])]
    return (a, b), (c, d)


def chunk_of(items, j):
    at = [j >= item["off"] for item in items[1:]]

    def choose(vals):
        v = vals[0]
        for later, val in zip(at, vals[1:]):
            v = jnp.where(later, val, v)
        return v

    def get(k):
        return choose([item[k] for item in items])

    r = jnp.clip(j - get("off") + get("base"), 0, RC - 1)
    return get, choose(list(range(len(items)))), r


def split(x):
    hi = x.astype(BF)
    return hi, (x - hi.astype(F32)).astype(BF)


def dot(a, b):
    return jnp.dot(a, b, preferred_element_type=F32)


def transforms(tab_ref, kre_ref, kim_ref):
    def left(zs, inv):
        hi, lo = tab_ref[2 - 2 * inv], tab_ref[3 - 2 * inv]
        out = []
        for z in zs:
            h, l = split(jnp.concatenate(z, axis=0))
            y = dot(hi, jnp.concatenate([h, l], axis=1))
            y = y[:, :PS] + y[:, PS:] + dot(lo, h)
            out.append((y[:PS], y[PS:]))
        return out

    def right(zs, inv):
        hi, lo = tab_ref[2 * inv], tab_ref[2 * inv + 1]
        out = []
        for z in zs:
            h, l = split(jnp.concatenate(z, axis=1))
            y = dot(h, hi) + dot(l, hi) + dot(h, lo)
            out.append((y[:, :PS], y[:, PS:]))
        return out

    def forward(zs):
        return right(left(zs, 0), 0)

    def backward(zs):
        return left(right(zs, 1), 1)

    def kernel_product(z, sign):
        re, im = z
        kre, kim = kre_ref[...], kim_ref[...] * sign
        return re * kre - im * kim, re * kim + im * kre

    return forward, backward, kernel_product


def neighbours():
    me, n = lax.axis_index("ty"), lax.axis_size("ty")
    following, previous = lax.rem(me + 1, n), lax.rem(me + n - 1, n)
    even = lax.rem(me, 2) == 0
    peers = [jnp.where(even, following, previous), jnp.where(even, previous, following)]
    return peers, even, following, previous


def remote(src, dst, sends, receives, to):
    return pltpu.make_async_remote_copy(
        src_ref=src, dst_ref=dst, send_sem=sends, recv_sem=receives, device_id=to, device_id_type=MESH
    )


class Group:
    def __init__(self, g, works, even, tile_ref, w_ref, t_ref, stage_ref, g_ref, maths):
        self.items, self.tile, self.w, self.t = works[g], tile_ref, w_ref, t_ref
        self.stage, self.g, self.maths = stage_ref, g_ref, maths
        self.up = even if g == 0 else jnp.logical_not(even)
        self.row = lax.broadcasted_iota(I32, (PS, PS), 0)
        self.lane = lax.broadcasted_iota(I32, (PS, PS), 1)
        self.lane8 = lax.broadcasted_iota(I32, (SUB, PS), 1)
        self.last = tile_ref[0].shape[0] - 1

    def ours(self, item):
        signed = self.row * jnp.where(self.up, 1, -1)
        return signed >= jnp.where(self.up, item["row"], 1 - item["row"])

    def object_of(self, s, got):
        at = RC
        for part in got:
            self.stage[pl.ds(at, part.shape[1])] = part[s]
            at += part.shape[1]
        for u, item in enumerate(self.items):
            here, after = item["block"], jnp.minimum(item["block"] + 1, self.last)
            start = RC + item["off"] - item["base"]
            mine = self.ours(item)
            for b in range(2):
                own = jnp.where(
                    self.lane >= item["lane"],
                    self.tile[s][here, b].reshape(PS, PS),
                    self.tile[s][after, b].reshape(PS, PS),
                )
                rest = jnp.concatenate([self.stage[start + r, b] for r in range(RC)], axis=0)
                self.t[s, u, b] = jnp.where(mine, own, rest)

    def through(self, s):
        zs = []
        for u in range(len(self.items)):
            wre, wim, tre, tim = self.w[s, u, 0], self.w[s, u, 1], self.t[s, u, 0], self.t[s, u, 1]
            zs.append((wre * tre - wim * tim, wre * tim + wim * tre))
        return zs

    def start(self, probe_ref):
        for u, item in enumerate(self.items):
            down = item["row"] & (PS - 1)
            for b in range(2):
                self.w[0, u, b] = pltpu.roll(pltpu.roll(probe_ref[b], down, 0), item["lane"], 1)

    def ahead(self, arrive, got):
        forward, backward, kernel_product = self.maths

        for s in range(NS - 1):
            arrive(s)
            self.object_of(s, got)
            zs = [kernel_product(z, 1.0) for z in forward(self.through(s))]
            for u, z in enumerate(backward(zs)):
                self.w[s + 1, u, 0], self.w[s + 1, u, 1] = z
        arrive(NS - 1)
        self.object_of(NS - 1, got)

    def back(self, length, pattern_of, pack, give, keep, write=None):
        forward, backward, kernel_product = self.maths
        items = self.items
        target = [
            jnp.where(self.lane8 >= item["lane"], item["block"], item["block"] + 1) for item in items
        ]
        grads = []
        for u, (re, im) in enumerate(forward(self.through(NS - 1))):
            pattern = pattern_of(u)
            live = jnp.where(items[u]["live"] > 0, 4.0, 0.0).astype(F32)
            f = (re * re + im * im - pattern) * live
            grads.append((re * f, im * f))
        grads = backward(grads)
        places = []
        for j in range(length):
            _, which, r = chunk_of(items, j)
            places.append((which, r))

        def deposit(s, grads):
            mines = []
            for u, (gre, gim) in enumerate(grads):
                mine = self.ours(items[u])
                wre, wim = self.w[s, u, 0], self.w[s, u, 1]
                both = []
                for b, val in enumerate((wre * gre + wim * gim, wre * gim - wim * gre)):
                    both.append(jnp.where(mine, val, 0.0).reshape(RC, SUB, PS))
                    self.g[u, b] = jnp.where(mine, 0.0, val).reshape(RC, SUB, PS)
                mines.append(both)
            for j, (which, r) in enumerate(places):
                for b in range(2):
                    pack(s, j, b, self.g[which, b, r])
            give(s).start()
            for k in range(self.last + 1):
                at_k = [(t == k)[None] for t in target]
                for b in range(2):
                    add = sum(jnp.where(m, v[b], 0.0) for m, v in zip(at_k, mines))
                    keep(k, s, b, add)
            if write is not None:
                write(s).start()

        def retreat(i, grads):
            s = NS - 1 - i
            deposit(s, grads)
            zs = []
            for u, (gre, gim) in enumerate(grads):
                tre, tim = self.t[s, u, 0], self.t[s, u, 1]
                zs.append((gre * tre + gim * tim, gim * tre - gre * tim))
            return tuple(backward([kernel_product(z, -1.0) for z in forward(zs)]))

        grads = lax.fori_loop(0, NS - 1, retreat, tuple(grads))
        deposit(0, grads)


def pack_rows(pack_ref, tile_ref, items, first, send, ready=lambda s: None):
    last = tile_ref[0].shape[0] - 1
    lane8 = lax.broadcasted_iota(I32, (SUB, PS), 1)
    table = []
    for j in range(pack_ref.shape[1]):
        get, _, r = chunk_of(items, first + j)
        block = get("block")
        table.append((block, jnp.minimum(block + 1, last), get("lane"), r))
    for s in range(NS):
        ready(s)
        for j, (here, after, shift, r) in enumerate(table):
            for b in range(2):
                pack_ref[s, j, b] = jnp.where(
                    lane8 >= shift, tile_ref[s][here, b, r], tile_ref[s][after, b, r]
                )
        send(s).start()


def first_kernel(
    count_ref, pos_hbm, tile_hbm, probe_hbm, phase_hbm, diff_hbm, tab_hbm,
    level_ref, table_ref, tile0, tile1, tile2, tile3, w0, t0, w1, t1, got1, dgot_ref,
    diff_ref, tab_ref, kre_ref, kim_ref,
    pos_ref, probe_ref, prev_ref, hello_ref, meta_ref, pack0, pack1, got0, stage_ref, dpack_ref,
    squad, all_ref,
    ts, ls, hs, fs, fr, ds, sq,
):
    peers, even, following, previous = neighbours()
    tiles, parts = lax.axis_size("ty"), lax.axis_size("grp")
    me = lax.axis_index("grp") * tiles + lax.axis_index("ty")
    squads = tiles * parts // SQUAD
    place, rank = me // SQUAD, lax.rem(me, SQUAD)
    blocks = tile_hbm.shape[4] // PS
    slots = pos_ref.shape[1]
    pack_ref, got_ref = (pack0, pack1), (got0, got1)

    def device(to):
        return {"grp": to // tiles, "ty": lax.rem(to, tiles)}

    mates = [device(place * SQUAD + lax.rem(rank + k, SQUAD)) for k in range(1, SQUAD)]
    fellows = [device(lax.rem(place + k, squads) * SQUAD + rank) for k in range(1, squads)]

    owns = [
        pltpu.make_async_copy(pos_hbm, pos_ref, hs.at[3]),
    ]
    for copy in owns:
        copy.start()
    barrier = pltpu.get_barrier_semaphore()
    for to in [{"ty": peer} for peer in peers] + mates + fellows:
        pl.semaphore_signal(barrier, inc=1, device_id=to, device_id_type=MESH)

    tile_ref = (tile0, tile1, tile2, tile3)

    def tile_copy(s, k):
        return pltpu.make_async_copy(
            tile_hbm.at[s, :, :, :, pl.ds(k * PS, PS)], tile_ref[s].at[k], ts.at[s, k]
        )

    for s in range(NS):
        for k in range(blocks):
            tile_copy(s, k).start()
    loads = [
        pltpu.make_async_copy(probe_hbm, probe_ref, ls.at[0]),
        pltpu.make_async_copy(phase_hbm, kre_ref, ls.at[1]),
        pltpu.make_async_copy(tab_hbm, tab_ref, ls.at[2]),
        pltpu.make_async_copy(diff_hbm, diff_ref, ls.at[3]),
    ]
    for copy in loads:
        copy.start()
    for copy in owns:
        copy.wait()
    count = count_ref[0]
    rows, cols = [pos_ref[0, i] for i in range(slots)], [pos_ref[1, i] for i in range(slots)]
    at = lax.broadcasted_iota(I32, (SUB, PS), 1)
    told = jnp.where(at == 2 * slots, count, 0)
    for i in range(slots):
        told = jnp.where(at == i, rows[i], told)
        told = jnp.where(at == slots + i, cols[i], told)
    hello_ref[...] = told
    pl.semaphore_wait(barrier, 2 + len(mates) + len(fellows))
    hello = remote(hello_ref, prev_ref, hs.at[0], hs.at[1], {"ty": following})
    hello.start()

    def fetch(g, s):
        return remote(pack_ref[g].at[s], got_ref[g].at[s], fs.at[g, s], fr.at[g, s], {"ty": peers[g]})

    patterns = remote(dpack_ref, dgot_ref, ds.at[0], ds.at[1], {"ty": following})

    mine = assign(rows, cols, count, even)
    down_own = mine[1]
    squad[rank] = jnp.zeros((1, PS), I32) + jnp.where(even, 0, mine[2])
    shouts = [remote(squad.at[rank], squad.at[rank], sq.at[0], sq.at[1], to) for to in mates]
    for copy in shouts:
        copy.start()

    def send_rows(g, items, ready=lambda s: None):
        pack_rows(pack_ref[g], tile_ref, items[: ITEMS[g]], 0, functools.partial(fetch, g), ready)

    def loaded(s):
        for k in range(blocks):
            tile_copy(s, k).wait()

    @pl.when(even)
    def _():
        send_rows(0, down_own, loaded)

    @pl.when(jnp.logical_not(even))
    def _():
        send_rows(1, down_own, loaded)

    hello.wait()
    learn = pltpu.make_async_copy(prev_ref, meta_ref, hs.at[2])
    learn.start()
    for copy in loads:
        copy.wait()
    for u in range(ITEMS[1]):
        dpack_ref[u] = diff_ref[down_own[u]["slot"]]
    learn.wait()
    prev = assign(*told_slots(meta_ref, slots), jnp.logical_not(even))

    @pl.when(even)
    def _():
        send_rows(1, prev[0])

    @pl.when(jnp.logical_not(even))
    def _():
        send_rows(0, prev[0])

    patterns.start()
    sends, works = listings(mine, prev, even)
    table_ref[...] = to_row(works, sends)
    phase = kre_ref[...]
    kre_ref[...] = jnp.cos(phase)
    kim_ref[...] = jnp.sin(phase)
    maths = transforms(tab_ref, kre_ref, kim_ref)
    chip = Group(0, works, even, tile_ref, w0, t0, stage_ref, None, maths)
    edge = Group(1, works, even, tile_ref, w1, t1, stage_ref, None, maths)
    chip.start(probe_ref)
    edge.start(probe_ref)

    def settle(ref, count, sem):
        part = ref.at[pl.ds(0, count)]
        pltpu.make_async_copy(part, part, sem).wait()

    settle(squad, SQUAD - 1, sq.at[1])
    settle(squad, SQUAD - 1, sq.at[0])
    all_ref[place] = jnp.max(squad[...], axis=0)
    for to in fellows:
        remote(all_ref.at[place], all_ref.at[place], sq.at[2], sq.at[3], to).start()

    chip.ahead(lambda s: fetch(0, s).wait_recv(), [got0])

    settle(all_ref, squads - 1, sq.at[3])
    settle(all_ref, squads - 1, sq.at[2])
    most = jnp.max(jnp.max(all_ref[...], axis=0))
    level = jnp.int32(0)
    for bound in LEVELS[:-1]:
        level = level + jnp.where(most > bound, 1, 0)
    level_ref[0] = level
    edge.ahead(lambda s: fetch(1, s).wait_recv(), [got1])
    for s in range(NS):
        for g in range(2):
            fetch(g, s).wait_send()
    patterns.wait()


def first_part(count, pos, tile, probe, phase, diff):
    tables = jnp.asarray(dft_parts())
    operands = [
        pltpu.with_memory_space_constraint(x, pltpu.HBM)
        for x in (pos, tile, probe, phase, diff, tables)
    ]
    blocks = tile.shape[4] // PS
    near, far = (NS, SHORT, 2, SUB, PS), (NS, LEVELS[0], 2, SUB, PS)
    few, most = ITEMS
    every = lax.axis_size("ty") * lax.axis_size("grp")
    dma = pltpu.SemaphoreType.DMA
    return pl.pallas_call(
        first_kernel,
        out_shape=(
            jax.ShapeDtypeStruct((1,), I32),
            jax.ShapeDtypeStruct((SUB, PS), I32),
        )
        + (jax.ShapeDtypeStruct((blocks, 2, RC, SUB, PS), F32),) * NS
        + (
            jax.ShapeDtypeStruct((NS, few, 2, PS, PS), F32),
            jax.ShapeDtypeStruct((NS, few, 2, PS, PS), F32),
            jax.ShapeDtypeStruct((NS, most, 2, PS, PS), F32),
            jax.ShapeDtypeStruct((NS, most, 2, PS, PS), F32),
            jax.ShapeDtypeStruct(far, F32),
            jax.ShapeDtypeStruct((most, PS, PS), F32),
            jax.ShapeDtypeStruct(diff.shape, F32),
            jax.ShapeDtypeStruct(tables.shape, BF),
            jax.ShapeDtypeStruct((PS, PS), F32),
            jax.ShapeDtypeStruct((PS, PS), F32),
        ),
        in_specs=[SMEM] + [pl.BlockSpec(memory_space=pltpu.HBM)] * len(operands),
        out_specs=(SMEM,) + (VMEM,) * (11 + NS),
        scratch_shapes=[
            pltpu.SMEM(pos.shape, I32),
            pltpu.VMEM((2, PS, PS), F32),
            pltpu.VMEM((SUB, PS), I32),
            pltpu.VMEM((SUB, PS), I32),
            pltpu.SMEM((SUB, PS), I32),
            pltpu.VMEM(near, F32),
            pltpu.VMEM(far, F32),
            pltpu.VMEM(near, F32),
            pltpu.VMEM((SHORT + 2 * RC, 2, SUB, PS), F32),
            pltpu.VMEM((most, PS, PS), F32),
            pltpu.VMEM((SQUAD, 1, PS), I32),
            pltpu.VMEM((every // SQUAD, 1, PS), I32),
            dma((NS, blocks)),
            dma((4,)),
            dma((5,)),
            dma((2, NS)),
            dma((2, NS)),
            dma((2,)),
            dma((4,)),
        ],
        compiler_params=pltpu.CompilerParams(
            collective_id=0, has_side_effects=True, vmem_limit_bytes=20 << 20
        ),
        cost_estimate=pl.CostEstimate(flops=5 * 10**9, bytes_accessed=5 * 10**6, transcendentals=0),
    )(count, *operands)


def second_kernel(
    length, table_ref, tile0, tile1, tile2, tile3, w0, t0, wa, ta, got_ref, dgot_ref, diff_ref,
    tab_ref, kre_ref, kim_ref,
    sum_hbm, near_hbm, far_hbm,
    table_s, stage_ref, g_ref, gpack0, gpack1, sum_ref, sem, gs_sem, gr_sem, out_sem, *more,
):
    peers, even, _, _ = neighbours()
    tile_ref = (tile0, tile1, tile2, tile3)
    barrier = pltpu.get_barrier_semaphore()
    for peer in peers:
        pl.semaphore_signal(barrier, inc=1, device_id={"ty": peer}, device_id_type=MESH)
    learn = pltpu.make_async_copy(table_ref, table_s, sem.at[0])
    learn.start()
    learn.wait()
    works, sends = from_row(table_s)
    pl.semaphore_wait(barrier, 2)

    gpacks, landings = (gpack0, gpack1), (near_hbm, far_hbm)

    def give(g, s):
        landing = landings[g].at[s, pl.ds(0, gpacks[g].shape[1])]
        return remote(gpacks[g].at[s], landing, gs_sem.at[g, s], gr_sem.at[g, s], {"ty": peers[g]})

    def pack(g, s, j, b, val):
        gpacks[g][s, 2 * j + b] = val

    def keep(g, k, s, b, val):
        if g == 1:
            sum_ref[s, b, :, :, k * PS : (k + 1) * PS] = val
        else:
            sum_ref[s, b, :, :, k * PS : (k + 1) * PS] += val

    def write(s):
        return pltpu.make_async_copy(sum_ref.at[s], sum_hbm.at[s], out_sem.at[s])

    maths = transforms(tab_ref, kre_ref, kim_ref)
    had = got_ref.shape[1]
    if length > had:
        wb, tb, pack_ref, rest_ref, fs, fr = more

        def fetch(s):
            return remote(pack_ref.at[s], rest_ref.at[s], fs.at[s], fr.at[s], {"ty": peers[1]})

        pack_rows(pack_ref, tile_ref, sends[1], had, fetch)
        edge = Group(1, works, even, tile_ref, wb, tb, stage_ref, g_ref, maths)
        wb[0] = wa[0]
        edge.ahead(lambda s: fetch(s).wait_recv(), [got_ref, rest_ref])
        for s in range(NS):
            fetch(s).wait_send()
    else:
        edge = Group(1, works, even, tile_ref, wa, ta, stage_ref, g_ref, maths)

    def pattern_of(group, u):
        return jnp.where(group.up, diff_ref[group.items[u]["slot"]], dgot_ref[u])

    chip = Group(0, works, even, tile_ref, w0, t0, stage_ref, g_ref, maths)
    for g, group, size, done in ((1, edge, length, None), (0, chip, SHORT, write)):
        group.back(
            size,
            functools.partial(pattern_of, group),
            functools.partial(pack, g),
            functools.partial(give, g),
            functools.partial(keep, g),
            done,
        )
    for s in range(NS):
        write(s).wait()
        for g in range(2):
            give(g, s).wait_send()
            give(g, s).wait_recv()


def second_part(level, *operands):
    tile, got = operands[1], operands[5 + NS]
    length, had = LEVELS[level], got.shape[1]
    full = (NS, 2, RC, SUB, tile.shape[0] * PS)
    most = ITEMS[1]
    dma = pltpu.SemaphoreType.DMA
    scratch = [
        pltpu.SMEM((SUB, PS), I32),
        pltpu.VMEM((length + 2 * RC, 2, SUB, PS), F32),
        pltpu.VMEM((most, 2, RC, SUB, PS), F32),
        pltpu.VMEM((NS, 2 * SHORT, SUB, PS), F32),
        pltpu.VMEM((NS, 2 * length, SUB, PS), F32),
        pltpu.VMEM(full, F32),
        dma((1,)),
        dma((2, NS)),
        dma((2, NS)),
        dma((NS,)),
    ]
    if length > had:
        scratch += [
            pltpu.VMEM((NS, most, 2, PS, PS), F32),
            pltpu.VMEM((NS, most, 2, PS, PS), F32),
            pltpu.VMEM((NS, length - had, 2, SUB, PS), F32),
            pltpu.VMEM((NS, length - had, 2, SUB, PS), F32),
            dma((NS,)),
            dma((NS,)),
        ]
    return pl.pallas_call(
        functools.partial(second_kernel, length),
        out_shape=(
            jax.ShapeDtypeStruct(full, F32),
            jax.ShapeDtypeStruct((NS, 2 * SHORT, SUB, PS), F32),
            jax.ShapeDtypeStruct((NS, 2 * LEVELS[-1], SUB, PS), F32),
        ),
        in_specs=[VMEM] * len(operands),
        out_specs=(pl.BlockSpec(memory_space=pltpu.HBM),) * 3,
        scratch_shapes=scratch,
        compiler_params=pltpu.CompilerParams(
            collective_id=1 + level, has_side_effects=True, vmem_limit_bytes=20 << 20
        ),
        cost_estimate=pl.CostEstimate(flops=3 * 10**9, bytes_accessed=5 * 10**6, transcendentals=0),
    )(*operands)


def place_kernel(table_ref, sum_hbm, near_hbm, far_hbm, out_hbm, sum_ref, near_ref, far_ref, table_s, sems):
    blocks = sum_ref.shape[4] // PS
    learn = pltpu.make_async_copy(table_ref, table_s, sems.at[0])
    arrive = [
        pltpu.make_async_copy(near_hbm, near_ref, sems.at[1]),
        pltpu.make_async_copy(far_hbm, far_ref, sems.at[2]),
    ]
    reads = [pltpu.make_async_copy(sum_hbm.at[s], sum_ref.at[s], sems.at[3 + s]) for s in range(NS)]
    for copy in [learn] + arrive + reads:
        copy.start()
    learn.wait()

    def theirs(g, s, j, b):
        return (near_ref, far_ref)[g][s, 2 * j + b]

    _, sends = from_row(table_s)
    for copy in arrive:
        copy.wait()
    lane8 = lax.broadcasted_iota(I32, (SUB, PS), 1)
    copies = []
    for pair in (range(s, s + 2) for s in range(0, NS, 2)):
        for s in pair:
            reads[s].wait()
        for g in range(2):
            for item in sends[g]:
                block, shift = item["block"], item["lane"]
                here = pl.ds(pl.multiple_of(block * PS, PS), PS)
                after = pl.ds(pl.multiple_of(jnp.minimum(block + 1, blocks - 1) * PS, PS), PS)

                def add(i, carry):
                    r, j = item["base"] + i, item["off"] + i
                    planes = [(s, b) for s in pair for b in range(2)]
                    got = [theirs(g, s, j, b) for s, b in planes]
                    old = [sum_ref[s, b, r, :, here] for s, b in planes]
                    for (s, b), x, y in zip(planes, old, got):
                        sum_ref[s, b, r, :, here] = x + jnp.where(lane8 >= shift, y, 0.0)
                    old = [sum_ref[s, b, r, :, after] for s, b in planes]
                    for (s, b), x, y in zip(planes, old, got):
                        sum_ref[s, b, r, :, after] = x + jnp.where(lane8 >= shift, 0.0, y)
                    return carry

                lax.fori_loop(0, item["n"], add, 0)
        for s in pair:
            copy = pltpu.make_async_copy(sum_ref.at[s], out_hbm.at[s], sems.at[3 + NS + s])
            copy.start()
            copies.append(copy)
    for copy in copies:
        copy.wait()


def place(table, total, near, far):
    hbm = pl.BlockSpec(memory_space=pltpu.HBM)
    return pl.pallas_call(
        place_kernel,
        in_specs=[VMEM] + [hbm] * 3,
        out_specs=pl.BlockSpec(memory_space=pltpu.HBM),
        out_shape=jax.ShapeDtypeStruct(total.shape, F32),
        scratch_shapes=[
            pltpu.VMEM(total.shape, F32),
            pltpu.VMEM(near.shape, F32),
            pltpu.VMEM(far.shape, F32),
            pltpu.SMEM((SUB, PS), I32),
            pltpu.SemaphoreType.DMA((3 + 2 * NS,)),
        ],
        compiler_params=pltpu.CompilerParams(vmem_limit_bytes=16 << 20),
        cost_estimate=pl.CostEstimate(flops=10**6, bytes_accessed=7 * 10**6, transcendentals=0),
    )(table, *[pltpu.with_memory_space_constraint(x, pltpu.HBM) for x in (total, near, far)])


def per_device(tile_object, probe_wave, propagator_phase, diffraction, positions, counts):
    width = tile_object.shape[3]
    pos = positions.T
    tile = tile_object.reshape(NS, 2, RC, SUB, width)
    level, table, *rest = first_part(
        counts, pos, tile, probe_wave, propagator_phase, diffraction
    )

    def branch(i):
        return lambda *args: second_part(i, *args)

    total, near, far = lax.switch(level[0], [branch(i) for i in range(len(LEVELS))], table, *rest)
    return place(table, total, near, far).reshape(tile_object.shape)


def solution(mesh):
    in_specs = (
        P(None, None, ("grp", "ty"), None),
        P(),
        P(),
        P(("grp", "ty"), None, None),
        P(("grp", "ty"), None),
        P(("grp", "ty")),
    )
    out_specs = P(None, None, ("grp", "ty"), None)
    return jax.shard_map(
        per_device, mesh=mesh, in_specs=in_specs, out_specs=out_specs, check_vma=False
    )
```

```python
import functools

import jax
import jax.numpy as jnp
import numpy as np
from jax import lax
from jax.experimental import pallas as pl
from jax.experimental.pallas import tpu as pltpu
from jax.sharding import PartitionSpec as P

PS = 128
NS = 4
SUB = 8
RC = PS // SUB
ITEMS = (2, 3)
SHORT = 2 * RC
LEVELS = (15, 17, 20)
SQUAD = 4
BF = jnp.bfloat16
F32 = jnp.float32
I32 = jnp.int32
VMEM = pl.BlockSpec(memory_space=pltpu.VMEM)
SMEM = pl.BlockSpec(memory_space=pltpu.SMEM)
MESH = pl.DeviceIdType.MESH


def dft_parts():
    k = np.arange(PS)
    ang = (np.outer(k, k) % PS) * (2.0 * np.pi / PS)
    c = np.cos(ang) / np.sqrt(PS)
    s = -np.sin(ang) / np.sqrt(PS)
    forward = np.block([[c, s], [-s, c]]).astype(np.float32)
    inverse = np.block([[c, -s], [s, c]]).astype(np.float32)
    parts = []
    for m in (forward, inverse):
        hi = m.astype(BF)
        lo = (m - hi.astype(np.float32)).astype(BF)
        parts += [hi, lo]
    return np.stack(parts)


def pick(flag, a, b):
    return {k: jnp.where(flag, a[k], b[k]) for k in a}


def assign(rows, cols, count, even):
    most = jnp.where(even, ITEMS[0], ITEMS[1])
    slots = len(rows)
    key = [jnp.where(i < count, rows[i], 1000) for i in range(slots)]
    rank = []
    for i in range(slots):
        r = jnp.int32(0)
        for j in range(slots):
            if j != i:
                ahead = key[j] <= key[i] if j < i else key[j] < key[i]
                r = r + jnp.where(ahead, 1, 0)
        rank.append(r)

    def ordered(vals):
        out = []
        for r in range(slots):
            v = jnp.int32(0)
            for i in range(slots):
                v = v + jnp.where(rank[i] == r, vals[i], 0)
            out.append(v)
        return out

    row, col, slot = ordered(rows), ordered(cols), ordered([jnp.int32(i) for i in range(slots)])
    above = [(row[r] + (SUB - 1)) >> 3 for r in range(slots)]
    below = [jnp.where(r < count, RC - (row[r] >> 3), 0) for r in range(slots)]
    best, cut = jnp.int32(10000), jnp.int32(0)
    for k in range(ITEMS[1] + 1):
        up = sum(above[:k], jnp.int32(0))
        down = sum(below[k:], jnp.int32(0))
        cost = jnp.maximum(up, down)
        bad = (k > count) | (k > most) | (count - k > most)
        cost = jnp.where(bad, 20000, cost)
        cut = jnp.where(cost < best, k, cut)
        best = jnp.minimum(cost, best)

    def listed(first, end, sizes, upward):
        items, off = [], jnp.int32(0)
        for u in range(ITEMS[1]):
            at = first + u
            live = at < end

            def take(vals):
                v = jnp.int32(0)
                for r in range(slots):
                    v = v + jnp.where(live & (at == r), vals[r], 0)
                return v

            n, c = take(sizes), take(col)
            items.append(
                dict(
                    live=jnp.where(live, 1, 0),
                    row=take(row) if upward else jnp.where(live, take(row), PS),
                    block=c >> 7,
                    lane=c & (PS - 1),
                    slot=take(slot),
                    off=off,
                    n=n,
                    base=jnp.int32(0) if upward else RC - n,
                )
            )
            off = off + n
        return items

    return listed(jnp.int32(0), cut, above, True), listed(cut, count, below, False), best


def told_slots(ref, slots):
    rows = [ref[0, i] for i in range(slots)]
    return rows, [ref[0, slots + i] for i in range(slots)], ref[0, 2 * slots]


def listings(own, prev, even):
    up_own, down_own, _ = own
    up_prev, down_prev, _ = prev
    sends = [
        [pick(even, a, b) for a, b in zip(down_own, up_prev)],
        [pick(even, a, b) for a, b in zip(up_prev, down_own)],
    ]
    works = [
        [pick(even, a, b) for a, b in zip(up_own, down_prev)],
        [pick(even, a, b) for a, b in zip(down_prev, up_own)],
    ]
    sends = [x[:m] for x, m in zip(sends, ITEMS)]
    works = [x[:m] for x, m in zip(works, ITEMS)]
    return sends, works


FIELDS = ("live", "row", "block", "lane", "slot", "off", "n", "base")


def to_row(works, sends):
    items = works[0] + works[1] + sends[0] + sends[1]
    at = lax.broadcasted_iota(I32, (SUB, PS), 1)
    row = jnp.zeros((SUB, PS), I32)
    for i, val in enumerate([item[f] for item in items for f in FIELDS]):
        row = jnp.where(at == i, val, row)
    return row


def from_row(ref):
    count = 2 * sum(ITEMS)
    items = [{f: ref[0, i * len(FIELDS) + k] for k, f in enumerate(FIELDS)} for i in range(count)]
    cuts = [0, ITEMS[0], sum(ITEMS), sum(ITEMS) + ITEMS[0], count]
    a, b, c, d = [items[i:j] for i, j in zip(cuts[:-1], cuts[1:])]
    return (a, b), (c, d)


def chunk_of(items, j):
    at = [j >= item["off"] for item in items[1:]]

    def choose(vals):
        v = vals[0]
        for later, val in zip(at, vals[1:]):
            v = jnp.where(later, val, v)
        return v

    def get(k):
        return choose([item[k] for item in items])

    r = jnp.clip(j - get("off") + get("base"), 0, RC - 1)
    return get, choose(list(range(len(items)))), r


def split(x):
    hi = x.astype(BF)
    return hi, (x - hi.astype(F32)).astype(BF)


def dot(a, b):
    return jnp.dot(a, b, preferred_element_type=F32)


def transforms(tab_ref, kre_ref, kim_ref):
    def left(zs, inv):
        hi, lo = tab_ref[2 - 2 * inv], tab_ref[3 - 2 * inv]
        out = []
        for z in zs:
            h, l = split(jnp.concatenate(z, axis=0))
            y = dot(hi, jnp.concatenate([h, l], axis=1))
            y = y[:, :PS] + y[:, PS:] + dot(lo, h)
            out.append((y[:PS], y[PS:]))
        return out

    def right(zs, inv):
        hi, lo = tab_ref[2 * inv], tab_ref[2 * inv + 1]
        out = []
        for z in zs:
            h, l = split(jnp.concatenate(z, axis=1))
            y = dot(h, hi) + dot(l, hi) + dot(h, lo)
            out.append((y[:, :PS], y[:, PS:]))
        return out

    def forward(zs):
        return right(left(zs, 0), 0)

    def backward(zs):
        return left(right(zs, 1), 1)

    def kernel_product(z, sign):
        re, im = z
        kre, kim = kre_ref[...], kim_ref[...] * sign
        return re * kre - im * kim, re * kim + im * kre

    return forward, backward, kernel_product


def neighbours():
    me, n = lax.axis_index("ty"), lax.axis_size("ty")
    following, previous = lax.rem(me + 1, n), lax.rem(me + n - 1, n)
    even = lax.rem(me, 2) == 0
    peers = [jnp.where(even, following, previous), jnp.where(even, previous, following)]
    return peers, even, following, previous


def remote(src, dst, sends, receives, to):
    return pltpu.make_async_remote_copy(
        src_ref=src, dst_ref=dst, send_sem=sends, recv_sem=receives, device_id=to, device_id_type=MESH
    )


class Group:
    def __init__(self, g, works, even, tile_ref, w_ref, t_ref, stage_ref, g_ref, maths):
        self.items, self.tile, self.w, self.t = works[g], tile_ref, w_ref, t_ref
        self.stage, self.g, self.maths = stage_ref, g_ref, maths
        self.up = even if g == 0 else jnp.logical_not(even)
        self.row = lax.broadcasted_iota(I32, (PS, PS), 0)
        self.lane = lax.broadcasted_iota(I32, (PS, PS), 1)
        self.lane8 = lax.broadcasted_iota(I32, (SUB, PS), 1)
        self.last = tile_ref[0].shape[0] - 1

    def ours(self, item):
        signed = self.row * jnp.where(self.up, 1, -1)
        return signed >= jnp.where(self.up, item["row"], 1 - item["row"])

    def object_of(self, s, got):
        at = RC
        for part in got:
            self.stage[pl.ds(at, part.shape[1])] = part[s]
            at += part.shape[1]
        for u, item in enumerate(self.items):
            here, after = item["block"], jnp.minimum(item["block"] + 1, self.last)
            start = RC + item["off"] - item["base"]
            mine = self.ours(item)
            for b in range(2):
                own = jnp.where(
                    self.lane >= item["lane"],
                    self.tile[s][here, b].reshape(PS, PS),
                    self.tile[s][after, b].reshape(PS, PS),
                )
                rest = jnp.concatenate([self.stage[start + r, b] for r in range(RC)], axis=0)
                self.t[s, u, b] = jnp.where(mine, own, rest)

    def through(self, s):
        zs = []
        for u in range(len(self.items)):
            wre, wim, tre, tim = self.w[s, u, 0], self.w[s, u, 1], self.t[s, u, 0], self.t[s, u, 1]
            zs.append((wre * tre - wim * tim, wre * tim + wim * tre))
        return zs

    def start(self, probe_ref):
        for u, item in enumerate(self.items):
            down = item["row"] & (PS - 1)
            for b in range(2):
                self.w[0, u, b] = pltpu.roll(pltpu.roll(probe_ref[b], down, 0), item["lane"], 1)

    def ahead(self, arrive, got):
        forward, backward, kernel_product = self.maths

        for s in range(NS - 1):
            arrive(s)
            self.object_of(s, got)
            zs = [kernel_product(z, 1.0) for z in forward(self.through(s))]
            for u, z in enumerate(backward(zs)):
                self.w[s + 1, u, 0], self.w[s + 1, u, 1] = z
        arrive(NS - 1)
        self.object_of(NS - 1, got)

    def back(self, length, pattern_of, pack, give, keep, write=None):
        forward, backward, kernel_product = self.maths
        items = self.items
        target = [
            jnp.where(self.lane8 >= item["lane"], item["block"], item["block"] + 1) for item in items
        ]
        grads = []
        for u, (re, im) in enumerate(forward(self.through(NS - 1))):
            pattern = pattern_of(u)
            live = jnp.where(items[u]["live"] > 0, 4.0, 0.0).astype(F32)
            f = (re * re + im * im - pattern) * live
            grads.append((re * f, im * f))
        grads = backward(grads)
        places = []
        for j in range(length):
            _, which, r = chunk_of(items, j)
            places.append((which, r))

        def deposit(s, grads):
            mines = []
            for u, (gre, gim) in enumerate(grads):
                mine = self.ours(items[u])
                wre, wim = self.w[s, u, 0], self.w[s, u, 1]
                both = []
                for b, val in enumerate((wre * gre + wim * gim, wre * gim - wim * gre)):
                    both.append(jnp.where(mine, val, 0.0).reshape(RC, SUB, PS))
                    self.g[u, b] = jnp.where(mine, 0.0, val).reshape(RC, SUB, PS)
                mines.append(both)
            for j, (which, r) in enumerate(places):
                for b in range(2):
                    pack(s, j, b, self.g[which, b, r])
            give(s).start()
            for k in range(self.last + 1):
                at_k = [(t == k)[None] for t in target]
                for b in range(2):
                    add = sum(jnp.where(m, v[b], 0.0) for m, v in zip(at_k, mines))
                    keep(k, s, b, add)
            if write is not None:
                write(s).start()

        def retreat(i, grads):
            s = NS - 1 - i
            deposit(s, grads)
            zs = []
            for u, (gre, gim) in enumerate(grads):
                tre, tim = self.t[s, u, 0], self.t[s, u, 1]
                zs.append((gre * tre + gim * tim, gim * tre - gre * tim))
            return tuple(backward([kernel_product(z, -1.0) for z in forward(zs)]))

        grads = lax.fori_loop(0, NS - 1, retreat, tuple(grads))
        deposit(0, grads)


def pack_rows(pack_ref, tile_ref, items, first, send, ready=lambda s: None):
    last = tile_ref[0].shape[0] - 1
    lane8 = lax.broadcasted_iota(I32, (SUB, PS), 1)
    table = []
    for j in range(pack_ref.shape[1]):
        get, _, r = chunk_of(items, first + j)
        block = get("block")
        table.append((block, jnp.minimum(block + 1, last), get("lane"), r))
    for s in range(NS):
        ready(s)
        for j, (here, after, shift, r) in enumerate(table):
            for b in range(2):
                pack_ref[s, j, b] = jnp.where(
                    lane8 >= shift, tile_ref[s][here, b, r], tile_ref[s][after, b, r]
                )
        send(s).start()


def first_kernel(
    count_ref, pos_hbm, tile_hbm, probe_hbm, phase_hbm, diff_hbm, tab_hbm,
    level_ref, table_ref, tile0, tile1, tile2, tile3, w0, t0, w1, t1, got1, dgot_ref,
    diff_ref, tab_ref, kre_ref, kim_ref,
    pos_ref, probe_ref, prev_ref, hello_ref, meta_ref, pack0, pack1, got0, stage_ref, dpack_ref,
    squad, all_ref,
    ts, ls, hs, fs, fr, ds, sq,
):
    peers, even, following, previous = neighbours()
    tiles, parts = lax.axis_size("ty"), lax.axis_size("grp")
    me = lax.axis_index("grp") * tiles + lax.axis_index("ty")
    squads = tiles * parts // SQUAD
    place, rank = me // SQUAD, lax.rem(me, SQUAD)
    blocks = tile_hbm.shape[4] // PS
    slots = pos_ref.shape[1]
    pack_ref, got_ref = (pack0, pack1), (got0, got1)

    def device(to):
        return {"grp": to // tiles, "ty": lax.rem(to, tiles)}

    mates = [device(place * SQUAD + lax.rem(rank + k, SQUAD)) for k in range(1, SQUAD)]
    fellows = [device(lax.rem(place + k, squads) * SQUAD + rank) for k in range(1, squads)]

    owns = [
        pltpu.make_async_copy(pos_hbm, pos_ref, hs.at[3]),
    ]
    for copy in owns:
        copy.start()
    barrier = pltpu.get_barrier_semaphore()
    for to in [{"ty": peer} for peer in peers] + mates + fellows:
        pl.semaphore_signal(barrier, inc=1, device_id=to, device_id_type=MESH)

    tile_ref = (tile0, tile1, tile2, tile3)

    def tile_copy(s, k):
        return pltpu.make_async_copy(
            tile_hbm.at[s, :, :, :, pl.ds(k * PS, PS)], tile_ref[s].at[k], ts.at[s, k]
        )

    for s in range(NS):
        for k in range(blocks):
            tile_copy(s, k).start()
    loads = [
        pltpu.make_async_copy(probe_hbm, probe_ref, ls.at[0]),
        pltpu.make_async_copy(phase_hbm, kre_ref, ls.at[1]),
        pltpu.make_async_copy(tab_hbm, tab_ref, ls.at[2]),
        pltpu.make_async_copy(diff_hbm, diff_ref, ls.at[3]),
    ]
    for copy in loads:
        copy.start()
    for copy in owns:
        copy.wait()
    count = count_ref[0]
    rows, cols = [pos_ref[0, i] for i in range(slots)], [pos_ref[1, i] for i in range(slots)]
    at = lax.broadcasted_iota(I32, (SUB, PS), 1)
    told = jnp.where(at == 2 * slots, count, 0)
    for i in range(slots):
        told = jnp.where(at == i, rows[i], told)
        told = jnp.where(at == slots + i, cols[i], told)
    hello_ref[...] = told
    pl.semaphore_wait(barrier, 2 + len(mates) + len(fellows))
    hello = remote(hello_ref, prev_ref, hs.at[0], hs.at[1], {"ty": following})
    hello.start()

    def fetch(g, s):
        return remote(pack_ref[g].at[s], got_ref[g].at[s], fs.at[g, s], fr.at[g, s], {"ty": peers[g]})

    patterns = remote(dpack_ref, dgot_ref, ds.at[0], ds.at[1], {"ty": following})

    mine = assign(rows, cols, count, even)
    down_own = mine[1]
    squad[rank] = jnp.zeros((1, PS), I32) + jnp.where(even, 0, mine[2])
    shouts = [remote(squad.at[rank], squad.at[rank], sq.at[0], sq.at[1], to) for to in mates]
    for copy in shouts:
        copy.start()

    def send_rows(g, items, ready=lambda s: None):
        pack_rows(pack_ref[g], tile_ref, items[: ITEMS[g]], 0, functools.partial(fetch, g), ready)

    def loaded(s):
        for k in range(blocks):
            tile_copy(s, k).wait()

    @pl.when(even)
    def _():
        send_rows(0, down_own, loaded)

    @pl.when(jnp.logical_not(even))
    def _():
        send_rows(1, down_own, loaded)

    hello.wait()
    learn = pltpu.make_async_copy(prev_ref, meta_ref, hs.at[2])
    learn.start()
    for copy in loads:
        copy.wait()
    for u in range(ITEMS[1]):
        dpack_ref[u] = diff_ref[down_own[u]["slot"]]
    learn.wait()
    prev = assign(*told_slots(meta_ref, slots), jnp.logical_not(even))

    @pl.when(even)
    def _():
        send_rows(1, prev[0])

    @pl.when(jnp.logical_not(even))
    def _():
        send_rows(0, prev[0])

    patterns.start()
    sends, works = listings(mine, prev, even)
    table_ref[...] = to_row(works, sends)
    phase = kre_ref[...]
    kre_ref[...] = jnp.cos(phase)
    kim_ref[...] = jnp.sin(phase)
    maths = transforms(tab_ref, kre_ref, kim_ref)
    chip = Group(0, works, even, tile_ref, w0, t0, stage_ref, None, maths)
    edge = Group(1, works, even, tile_ref, w1, t1, stage_ref, None, maths)
    chip.start(probe_ref)
    edge.start(probe_ref)

    def settle(ref, count, sem):
        part = ref.at[pl.ds(0, count)]
        pltpu.make_async_copy(part, part, sem).wait()

    settle(squad, SQUAD - 1, sq.at[1])
    settle(squad, SQUAD - 1, sq.at[0])
    all_ref[place] = jnp.max(squad[...], axis=0)
    for to in fellows:
        remote(all_ref.at[place], all_ref.at[place], sq.at[2], sq.at[3], to).start()

    chip.ahead(lambda s: fetch(0, s).wait_recv(), [got0])

    settle(all_ref, squads - 1, sq.at[3])
    settle(all_ref, squads - 1, sq.at[2])
    most = jnp.max(jnp.max(all_ref[...], axis=0))
    level = jnp.int32(0)
    for bound in LEVELS[:-1]:
        level = level + jnp.where(most > bound, 1, 0)
    level_ref[0] = level
    edge.ahead(lambda s: fetch(1, s).wait_recv(), [got1])
    for s in range(NS):
        for g in range(2):
            fetch(g, s).wait_send()
    patterns.wait()


def first_part(count, pos, tile, probe, phase, diff):
    tables = jnp.asarray(dft_parts())
    operands = [
        pltpu.with_memory_space_constraint(x, pltpu.HBM)
        for x in (pos, tile, probe, phase, diff, tables)
    ]
    blocks = tile.shape[4] // PS
    near, far = (NS, SHORT, 2, SUB, PS), (NS, LEVELS[0], 2, SUB, PS)
    few, most = ITEMS
    every = lax.axis_size("ty") * lax.axis_size("grp")
    dma = pltpu.SemaphoreType.DMA
    return pl.pallas_call(
        first_kernel,
        out_shape=(
            jax.ShapeDtypeStruct((1,), I32),
            jax.ShapeDtypeStruct((SUB, PS), I32),
        )
        + (jax.ShapeDtypeStruct((blocks, 2, RC, SUB, PS), F32),) * NS
        + (
            jax.ShapeDtypeStruct((NS, few, 2, PS, PS), F32),
            jax.ShapeDtypeStruct((NS, few, 2, PS, PS), F32),
            jax.ShapeDtypeStruct((NS, most, 2, PS, PS), F32),
            jax.ShapeDtypeStruct((NS, most, 2, PS, PS), F32),
            jax.ShapeDtypeStruct(far, F32),
            jax.ShapeDtypeStruct((most, PS, PS), F32),
            jax.ShapeDtypeStruct(diff.shape, F32),
            jax.ShapeDtypeStruct(tables.shape, BF),
            jax.ShapeDtypeStruct((PS, PS), F32),
            jax.ShapeDtypeStruct((PS, PS), F32),
        ),
        in_specs=[SMEM] + [pl.BlockSpec(memory_space=pltpu.HBM)] * len(operands),
        out_specs=(SMEM,) + (VMEM,) * (11 + NS),
        scratch_shapes=[
            pltpu.SMEM(pos.shape, I32),
            pltpu.VMEM((2, PS, PS), F32),
            pltpu.VMEM((SUB, PS), I32),
            pltpu.VMEM((SUB, PS), I32),
            pltpu.SMEM((SUB, PS), I32),
            pltpu.VMEM(near, F32),
            pltpu.VMEM(far, F32),
            pltpu.VMEM(near, F32),
            pltpu.VMEM((SHORT + 2 * RC, 2, SUB, PS), F32),
            pltpu.VMEM((most, PS, PS), F32),
            pltpu.VMEM((SQUAD, 1, PS), I32),
            pltpu.VMEM((every // SQUAD, 1, PS), I32),
            dma((NS, blocks)),
            dma((4,)),
            dma((5,)),
            dma((2, NS)),
            dma((2, NS)),
            dma((2,)),
            dma((4,)),
        ],
        compiler_params=pltpu.CompilerParams(
            collective_id=0, has_side_effects=True, vmem_limit_bytes=20 << 20
        ),
        cost_estimate=pl.CostEstimate(flops=5 * 10**9, bytes_accessed=5 * 10**6, transcendentals=0),
    )(count, *operands)


def second_kernel(
    length, table_ref, tile0, tile1, tile2, tile3, w0, t0, wa, ta, got_ref, dgot_ref, diff_ref,
    tab_ref, kre_ref, kim_ref,
    sum_hbm, near_hbm, far_hbm,
    table_s, stage_ref, g_ref, gpack0, gpack1, sum_ref, sem, gs_sem, gr_sem, out_sem, *more,
):
    peers, even, _, _ = neighbours()
    tile_ref = (tile0, tile1, tile2, tile3)
    barrier = pltpu.get_barrier_semaphore()
    for peer in peers:
        pl.semaphore_signal(barrier, inc=1, device_id={"ty": peer}, device_id_type=MESH)
    learn = pltpu.make_async_copy(table_ref, table_s, sem.at[0])
    learn.start()
    learn.wait()
    works, sends = from_row(table_s)
    pl.semaphore_wait(barrier, 2)

    gpacks, landings = (gpack0, gpack1), (near_hbm, far_hbm)

    def give(g, s):
        landing = landings[g].at[s, pl.ds(0, gpacks[g].shape[1])]
        return remote(gpacks[g].at[s], landing, gs_sem.at[g, s], gr_sem.at[g, s], {"ty": peers[g]})

    def pack(g, s, j, b, val):
        gpacks[g][s, 2 * j + b] = val

    def keep(g, k, s, b, val):
        if g == 1:
            sum_ref[s, b, :, :, k * PS : (k + 1) * PS] = val
        else:
            sum_ref[s, b, :, :, k * PS : (k + 1) * PS] += val

    def write(s):
        return pltpu.make_async_copy(sum_ref.at[s], sum_hbm.at[s], out_sem.at[s])

    maths = transforms(tab_ref, kre_ref, kim_ref)
    had = got_ref.shape[1]
    if length > had:
        wb, tb, pack_ref, rest_ref, fs, fr = more

        def fetch(s):
            return remote(pack_ref.at[s], rest_ref.at[s], fs.at[s], fr.at[s], {"ty": peers[1]})

        pack_rows(pack_ref, tile_ref, sends[1], had, fetch)
        edge = Group(1, works, even, tile_ref, wb, tb, stage_ref, g_ref, maths)
        wb[0] = wa[0]
        edge.ahead(lambda s: fetch(s).wait_recv(), [got_ref, rest_ref])
        for s in range(NS):
            fetch(s).wait_send()
    else:
        edge = Group(1, works, even, tile_ref, wa, ta, stage_ref, g_ref, maths)

    def pattern_of(group, u):
        return jnp.where(group.up, diff_ref[group.items[u]["slot"]], dgot_ref[u])

    chip = Group(0, works, even, tile_ref, w0, t0, stage_ref, g_ref, maths)
    for g, group, size, done in ((1, edge, length, None), (0, chip, SHORT, write)):
        group.back(
            size,
            functools.partial(pattern_of, group),
            functools.partial(pack, g),
            functools.partial(give, g),
            functools.partial(keep, g),
            done,
        )
    for s in range(NS):
        write(s).wait()
        for g in range(2):
            give(g, s).wait_send()
            give(g, s).wait_recv()


def second_part(level, *operands):
    tile, got = operands[1], operands[5 + NS]
    length, had = LEVELS[level], got.shape[1]
    full = (NS, 2, RC, SUB, tile.shape[0] * PS)
    most = ITEMS[1]
    dma = pltpu.SemaphoreType.DMA
    scratch = [
        pltpu.SMEM((SUB, PS), I32),
        pltpu.VMEM((length + 2 * RC, 2, SUB, PS), F32),
        pltpu.VMEM((most, 2, RC, SUB, PS), F32),
        pltpu.VMEM((NS, 2 * SHORT, SUB, PS), F32),
        pltpu.VMEM((NS, 2 * length, SUB, PS), F32),
        pltpu.VMEM(full, F32),
        dma((1,)),
        dma((2, NS)),
        dma((2, NS)),
        dma((NS,)),
    ]
    if length > had:
        scratch += [
            pltpu.VMEM((NS, most, 2, PS, PS), F32),
            pltpu.VMEM((NS, most, 2, PS, PS), F32),
            pltpu.VMEM((NS, length - had, 2, SUB, PS), F32),
            pltpu.VMEM((NS, length - had, 2, SUB, PS), F32),
            dma((NS,)),
            dma((NS,)),
        ]
    return pl.pallas_call(
        functools.partial(second_kernel, length),
        out_shape=(
            jax.ShapeDtypeStruct(full, F32),
            jax.ShapeDtypeStruct((NS, 2 * SHORT, SUB, PS), F32),
            jax.ShapeDtypeStruct((NS, 2 * LEVELS[-1], SUB, PS), F32),
        ),
        in_specs=[VMEM] * len(operands),
        out_specs=(pl.BlockSpec(memory_space=pltpu.HBM),) * 3,
        scratch_shapes=scratch,
        compiler_params=pltpu.CompilerParams(
            collective_id=1 + level, has_side_effects=True, vmem_limit_bytes=20 << 20
        ),
        cost_estimate=pl.CostEstimate(flops=3 * 10**9, bytes_accessed=5 * 10**6, transcendentals=0),
    )(*operands)


def place_kernel(table_ref, sum_hbm, near_hbm, far_hbm, out_hbm, sum_ref, near_ref, far_ref, table_s, sems):
    blocks = sum_ref.shape[4] // PS
    learn = pltpu.make_async_copy(table_ref, table_s, sems.at[0])
    arrive = [
        pltpu.make_async_copy(near_hbm, near_ref, sems.at[1]),
        pltpu.make_async_copy(far_hbm, far_ref, sems.at[2]),
    ]
    reads = [pltpu.make_async_copy(sum_hbm.at[s], sum_ref.at[s], sems.at[3 + s]) for s in range(NS)]
    for copy in [learn] + arrive + reads:
        copy.start()
    learn.wait()

    def theirs(g, s, j, b):
        return (near_ref, far_ref)[g][s, 2 * j + b]

    _, sends = from_row(table_s)
    for copy in arrive:
        copy.wait()
    lane8 = lax.broadcasted_iota(I32, (SUB, PS), 1)
    copies = []
    for pair in (range(s, s + 2) for s in range(0, NS, 2)):
        for s in pair:
            reads[s].wait()
        for g in range(2):
            for item in sends[g]:
                block, shift = item["block"], item["lane"]
                here = pl.ds(pl.multiple_of(block * PS, PS), PS)
                after = pl.ds(pl.multiple_of(jnp.minimum(block + 1, blocks - 1) * PS, PS), PS)

                def add(i, carry):
                    r, j = item["base"] + i, item["off"] + i
                    planes = [(s, b) for s in pair for b in range(2)]
                    got = [theirs(g, s, j, b) for s, b in planes]
                    old = [sum_ref[s, b, r, :, here] for s, b in planes]
                    for (s, b), x, y in zip(planes, old, got):
                        sum_ref[s, b, r, :, here] = x + jnp.where(lane8 >= shift, y, 0.0)
                    old = [sum_ref[s, b, r, :, after] for s, b in planes]
                    for (s, b), x, y in zip(planes, old, got):
                        sum_ref[s, b, r, :, after] = x + jnp.where(lane8 >= shift, 0.0, y)
                    return carry

                lax.fori_loop(0, item["n"], add, 0)
        for s in pair:
            copy = pltpu.make_async_copy(sum_ref.at[s], out_hbm.at[s], sems.at[3 + NS + s])
            copy.start()
            copies.append(copy)
    for copy in copies:
        copy.wait()


def place(table, total, near, far):
    hbm = pl.BlockSpec(memory_space=pltpu.HBM)
    return pl.pallas_call(
        place_kernel,
        in_specs=[VMEM] + [hbm] * 3,
        out_specs=pl.BlockSpec(memory_space=pltpu.HBM),
        out_shape=jax.ShapeDtypeStruct(total.shape, F32),
        scratch_shapes=[
            pltpu.VMEM(total.shape, F32),
            pltpu.VMEM(near.shape, F32),
            pltpu.VMEM(far.shape, F32),
            pltpu.SMEM((SUB, PS), I32),
            pltpu.SemaphoreType.DMA((3 + 2 * NS,)),
        ],
        compiler_params=pltpu.CompilerParams(vmem_limit_bytes=16 << 20),
        cost_estimate=pl.CostEstimate(flops=10**6, bytes_accessed=7 * 10**6, transcendentals=0),
    )(table, *[pltpu.with_memory_space_constraint(x, pltpu.HBM) for x in (total, near, far)])


def per_device(tile_object, probe_wave, propagator_phase, diffraction, positions, counts):
    width = tile_object.shape[3]
    pos = positions.T
    tile = tile_object.reshape(NS, 2, RC, SUB, width)
    level, table, *rest = first_part(
        counts, pos, tile, probe_wave, propagator_phase, diffraction
    )

    def branch(i):
        return lambda *args: second_part(i, *args)

    total, near, far = lax.switch(level[0], [branch(i) for i in range(len(LEVELS))], table, *rest)
    return place(table, total, near, far).reshape(tile_object.shape)


def solution(mesh):
    in_specs = (
        P(None, None, ("grp", "ty"), None),
        P(),
        P(),
        P(("grp", "ty"), None, None),
        P(("grp", "ty"), None),
        P(("grp", "ty")),
    )
    out_specs = P(None, None, ("grp", "ty"), None)
    return jax.shard_map(
        per_device, mesh=mesh, in_specs=in_specs, out_specs=out_specs, check_vma=False
    )
```
